32 devices in a mesh: dp: 8 (over y, x, core), tensor: 4 (over z).
Axes of the slice: x: 2, y: 2, z: 4, core: 2. Of those that a mesh axis runs over, the one named last changes fastest.
Arguments:
- tokens: bfloat16 [16384, 768], P(('dp', 'tensor')), may hold values from -6 to 6
- cotangent: bfloat16 [16384, 768], P(('dp', 'tensor')), may hold values from -6 to 6
- lengths: int32 [8], P('dp'), may hold values from 1025 to 2048, as said below
- query_weight: bfloat16 [768, 768], P('dp', 'tensor'), may hold values from -0.3125 to 0.3125
- key_weight: bfloat16 [768, 768], P('dp', 'tensor'), may hold values from -0.3125 to 0.3125
- value_weight: bfloat16 [768, 768], P('dp', 'tensor'), may hold values from -0.21875 to 0.21875
- query_bias: bfloat16 [64, 12], P('dp', 'tensor'), may hold values from -1.796875 to 1.796875
- value_bias: bfloat16 [64, 12], P('dp', 'tensor'), may hold values from -0.59765625 to 0.59765625
- output_weight: bfloat16 [768, 768], P('dp', 'tensor'), may hold values from -0.875 to 0.875
- output_bias: bfloat16 [768], P('dp'), may hold values from -1.796875 to 1.796875
- first_gain: bfloat16 [768], P('dp'), may hold values from 0.5 to 1.5
- first_shift: bfloat16 [768], P('dp'), may hold values from -1.796875 to 1.796875
- inner_weight: bfloat16 [768, 3072], P('dp', 'tensor'), may hold values from -0.21875 to 0.21875
- inner_bias: bfloat16 [64, 48], P('dp', 'tensor'), may hold values from -1.796875 to 1.796875
- outer_weight: bfloat16 [768, 3072], P('dp', 'tensor'), may hold values from -0.109375 to 0.109375
- outer_bias: bfloat16 [768], P('dp'), may hold values from -1.796875 to 1.796875
- second_gain: bfloat16 [768], P('dp'), may hold values from 0.5 to 1.5
- second_shift: bfloat16 [768], P('dp'), may hold values from -1.796875 to 1.796875
Outputs:
- layer_out: bfloat16 [16384, 768], P(('dp', 'tensor'))
- tokens_gradient: float32 [16384, 768], P(('dp', 'tensor'))
- query_weight_gradient: float32 [768, 768], P('dp', 'tensor')
- key_weight_gradient: float32 [768, 768], P('dp', 'tensor')
- value_weight_gradient: float32 [768, 768], P('dp', 'tensor')
- query_bias_gradient: float32 [64, 12], P('dp', 'tensor')
- value_bias_gradient: float32 [64, 12], P('dp', 'tensor')
- output_weight_gradient: float32 [768, 768], P('dp', 'tensor')
- output_bias_gradient: float32 [768], P('dp')
- first_gain_gradient: float32 [768], P('dp')
- first_shift_gradient: float32 [768], P('dp')
- inner_weight_gradient: float32 [768, 3072], P('dp', 'tensor')
- inner_bias_gradient: float32 [64, 48], P('dp', 'tensor')
- outer_weight_gradient: float32 [768, 3072], P('dp', 'tensor')
- outer_bias_gradient: float32 [768], P('dp')
- second_gain_gradient: float32 [768], P('dp')
- second_shift_gradient: float32 [768], P('dp')
The draws below stay inside these ranges and needn't reach their ends.
Inputs may be any that keep to these rules, and one draw needn't show every extreme that they name: lengths[s] is the number of valid tokens at the start of slot s; some slot is full and some holds exactly 1025.
All inputs are finite; a program needn't handle non-finite values.
Results may differ from the reference program's by a relative error of at most 0.014.
The reference program's roundings to bfloat16 on the way count: a program that leaves them out, or rounds other values in their place, can miss the bound.
Values may be sent and summed in bfloat16 or wider, within the bound.
No kernel may reach another device: no remote copies, remote signals or barrier semaphores. Data moves between devices by JAX's collectives and lax.ppermute only.
A program may use at most 128 MiB of HBM per device.

```python
import math
import jax
import jax.numpy as jnp
from jax import lax

D = 768
H = 12
HD = 64
FF = 3072
SLOT_LEN = 2048
SLOTS = 1
SEQS = 8
TOKENS = 16384
N_DP = 8


def draw_lengths(key, part):
    lower = SLOT_LEN // 2 + 1
    values = jax.random.randint(jax.random.fold_in(key, 11), (SEQS,), lower, SLOT_LEN + 1)
    first = jax.random.randint(jax.random.fold_in(key, 12), (), 0, SEQS)
    offset = jax.random.randint(jax.random.fold_in(key, 13), (), 1, SEQS)
    second = (first + offset) % SEQS
    values = values.at[first].set(SLOT_LEN)
    values = values.at[second].set(lower)
    return values.astype(jnp.int32)


def with_spikes(array, stream_key, source, target, parts, factor):
    def block_of(axis_at):
        return (jnp.arange(array.shape[axis_at]) // (array.shape[axis_at] // parts)).reshape((-1,) + (1,) * (array.ndim - 1 - axis_at))

    near = jax.random.permutation(stream_key, parts)[block_of(target)]
    far = (block_of(target) + parts // 2) % parts
    return jnp.where((block_of(source) == near) | (block_of(source) == far), factor * array, array)


def steps_of(rng, extent, split, smallest, largest):
    factor_of, own = 1.0, jax.random.fold_in(rng, 6)
    for axis_at, shards_of in split:
        draws = jnp.exp(jax.random.uniform(jax.random.fold_in(own, axis_at), (shards_of,), jnp.float32, smallest / len(split), largest / len(split)))
        factor_of = factor_of * jnp.repeat(draws, extent[axis_at] // shards_of).reshape([-1 if axis == axis_at else 1 for axis in range(len(extent))])
    return factor_of


def normal_values(rng, shape, scale, reach, split=(), kind=jnp.bfloat16):
    drawn = scale * jax.random.normal(rng, shape, jnp.float32)
    if split:
        drawn = drawn * steps_of(rng, shape, split, -0.22, 0.18)
    return jnp.clip(drawn, -reach, reach).astype(kind)


def bell_draw_with(key, dims, deviation, reach, shards, heavy, kind=jnp.bfloat16):
    entries = deviation * jax.random.normal(key, dims, jnp.float32)
    if shards:
        entries = entries * steps_of(key, dims, shards, -0.22, 0.18)
    return jnp.clip(with_spikes(entries, jax.random.fold_in(key, 3), *heavy), -reach, reach).astype(kind)


def setup_inputs(seed: int = 0) -> dict:
    streams_of = jax.random.split(jax.random.key(seed), 19)
    return {
        "tokens": normal_values(streams_of[0], (TOKENS, D), 1.0, 6.0, ((0, 32),)),
        "cotangent": bell_draw_with(streams_of[1], (TOKENS, D), 1.0, 6.0, ((0, 32),), (0, 1, 32, 2.75)),
        "lengths": draw_lengths(jax.random.fold_in(streams_of[18], 71), 0),
        "query_weight": normal_values(streams_of[3], (D, D), (D // 2) ** -0.5, 0.3125, ((0, 8), (1, 4))),
        "key_weight": normal_values(streams_of[4], (D, D), (D // 2) ** -0.5, 0.3125, ((0, 8), (1, 4))),
        "value_weight": normal_values(streams_of[5], (D, D), D ** -0.5, 0.21875, ((0, 8), (1, 4))),
        "query_bias": normal_values(streams_of[6], (HD, H), 0.3, 1.796875, ((0, 8), (1, 4))),
        "value_bias": normal_values(streams_of[7], (HD, H), 0.1, 0.59765625, ((0, 8), (1, 4))),
        "output_weight": normal_values(streams_of[8], (D, D), (D // 16) ** -0.5, 0.875, ((0, 8), (1, 4))),
        "output_bias": normal_values(streams_of[9], (D,), 0.3, 1.796875, ((0, 8),)),
        "first_gain": jnp.clip(1.0 + 0.1 * jax.random.normal(streams_of[10], (D,), jnp.float32), 0.5, 1.5).astype(jnp.bfloat16),
        "first_shift": normal_values(streams_of[11], (D,), 0.3, 1.796875, ((0, 8),)),
        "inner_weight": normal_values(streams_of[12], (D, FF), D ** -0.5, 0.21875, ((0, 8), (1, 4))),
        "inner_bias": normal_values(streams_of[13], (HD, FF // HD), 0.3, 1.796875, ((0, 8), (1, 4))),
        "outer_weight": normal_values(streams_of[14], (D, FF), FF ** -0.5, 0.109375, ((0, 8), (1, 4))),
        "outer_bias": normal_values(streams_of[15], (D,), 0.3, 1.796875, ((0, 8),)),
        "second_gain": jnp.clip(1.0 + 0.1 * jax.random.normal(streams_of[16], (D,), jnp.float32), 0.5, 1.5).astype(jnp.bfloat16),
        "second_shift": normal_values(streams_of[17], (D,), 0.3, 1.796875, ((0, 8),)),
    }


@jax.custom_vjp
def low(v):
    return lax.optimization_barrier(v.astype(jnp.bfloat16)).astype(jnp.float32)

@jax.custom_vjp
def low_back(v):
    return v

def low_keep(v):
    return (low(v), None)

def low_pass(kept, grad):
    return (grad,)

def back_keep(v):
    return (v, None)

def back_low(kept, grad):
    return (low(grad),)
low.defvjp(low_keep, low_pass)
low_back.defvjp(back_keep, back_low)
epsilon = 1e-05
negative = -1e+30

def matmul(left, right):
    return jnp.dot(left, right, precision=lax.Precision.HIGHEST)

def normalize(rows, gain, shift):
    center = rows - lax.optimization_barrier(jnp.mean(rows, axis=-1, keepdims=True))
    spread = lax.rsqrt(lax.optimization_barrier(jnp.mean(center * center, axis=-1, keepdims=True)) + epsilon)
    return center * spread * gain + shift

def attend_block(query_block, key, value, valid):
    scores = jnp.einsum('qhd,khd->hqk', query_block, key, precision=lax.Precision.HIGHEST)
    scores = low_back(scores * HD ** (-0.5))
    scores = jnp.where(valid[None, None, :], scores, negative)
    peak = lax.optimization_barrier(jnp.max(scores, axis=-1, keepdims=True))
    expo = jnp.exp(scores - peak)
    probs = expo / lax.optimization_barrier(jnp.sum(expo, axis=-1, keepdims=True))
    return jnp.einsum('hqk,khd->qhd', low(probs), value, precision=lax.Precision.HIGHEST)

def attend_slot(query, key, value, valid):
    block = math.gcd(SLOT_LEN, 512)
    blocks = query.reshape(SLOT_LEN // block, block, H, HD)
    checked = jax.checkpoint(attend_block)
    mixed = lax.map(lambda query_block: checked(query_block, key, value, valid), blocks)
    return mixed.reshape(SLOT_LEN, H * HD)

def layer(rows, params, valid_rows, key_valid):
    query_weight, key_weight, value_weight, query_bias, value_bias, output_weight, output_bias, first_gain, first_shift, inner_weight, inner_bias, outer_weight, outer_bias, second_gain, second_shift = params
    query = low(low_back(matmul(rows, query_weight)) + query_bias.T.reshape(-1))
    key = low(low_back(matmul(rows, key_weight)))
    value = low(low_back(matmul(rows, value_weight)) + value_bias.T.reshape(-1))
    shaped = (SLOTS, SLOT_LEN, H, HD)
    mixed = lax.map(lambda item: attend_slot(item[0], item[1], item[2], item[3]), (query.reshape(shaped), key.reshape(shaped), value.reshape(shaped), key_valid))
    mixed = low(low_back(mixed.reshape(SLOTS * SLOT_LEN, D)))
    attention = low_back(matmul(mixed, output_weight.T)) + output_bias
    hidden = normalize(rows + attention, first_gain, first_shift)
    inner = low_back(matmul(low(hidden), inner_weight)) + inner_bias.T.reshape(-1)
    active = low(jax.nn.gelu(inner, approximate=False))
    network = low_back(matmul(active, outer_weight.T)) + outer_bias
    return valid_rows[:, None] * normalize(hidden + network, second_gain, second_shift)

def reference(tokens, cotangent, lengths, query_weight, key_weight, value_weight, query_bias, value_bias, output_weight, output_bias, first_gain, first_shift, inner_weight, inner_bias, outer_weight, outer_bias, second_gain, second_shift):
    params = tuple((item.astype(jnp.float32) for item in (query_weight, key_weight, value_weight, query_bias, value_bias, output_weight, output_bias, first_gain, first_shift, inner_weight, inner_bias, outer_weight, outer_bias, second_gain, second_shift)))
    group_rows = SLOTS * SLOT_LEN
    inputs = tokens.astype(jnp.float32).reshape(N_DP, group_rows, D)
    incoming = cotangent.astype(jnp.float32).reshape(N_DP, group_rows, D)
    key_valid = jnp.arange(SLOT_LEN)[None, None, :] < lengths.reshape(N_DP, SLOTS)[:, :, None]

    def group(totals, item):
        rows, grad_rows, valid = item
        valid_rows = valid.reshape(-1).astype(jnp.float32)
        output, pull = jax.vjp(lambda inner_rows, inner_params: layer(inner_rows, inner_params, valid_rows, valid), rows, params)
        rows_grad, param_grads = pull(grad_rows)
        totals = jax.tree.map(jnp.add, totals, param_grads)
        return (totals, (output, rows_grad))
    zeros = jax.tree.map(jnp.zeros_like, params)
    totals, (outputs, rows_grads) = lax.scan(group, zeros, (inputs, incoming, key_valid))
    return (outputs.reshape(TOKENS, D).astype(jnp.bfloat16), rows_grads.reshape(TOKENS, D), totals[0], totals[1], totals[2], totals[3], totals[4], totals[5], totals[6], totals[7], totals[8], totals[9], totals[10], totals[11], totals[12], totals[13], totals[14])
```

```python
import functools
import math

import jax
import jax.numpy as jnp
from jax import lax
from jax.experimental import pallas as pl
from jax.experimental.pallas import tpu as pltpu
from jax.sharding import PartitionSpec as P

HD = 64
SLOT_LEN = 2048
EPS = 1e-05
NEG = -1e30
BF = jnp.bfloat16
F32 = jnp.float32
VMEM_LIMIT = 60 * 1024 * 1024


def dot(a, b, ca, cb):
    return lax.dot_general(a, b, (((ca,), (cb,)), ((), ())), preferred_element_type=F32)


def whole(shape):
    return pl.BlockSpec(shape, lambda *_: (0,) * len(shape))


def params():
    return pltpu.CompilerParams(vmem_limit_bytes=VMEM_LIMIT)


def swap(x, axis, mask):
    n = lax.axis_size(axis)
    return lax.ppermute(x, axis, [(i, i ^ mask) for i in range(n)])


def dp_groups():
    n, bit, groups = lax.axis_size("dp"), 2, []
    while bit < n:
        if bit * 2 < n:
            groups.append((bit, bit * 2, bit * 3))
            bit *= 4
        else:
            groups.append((bit,))
            bit *= 2
    return groups


def gather_tensor(piece):
    return [piece] + [swap(piece, "tensor", m) for m in range(1, lax.axis_size("tensor"))]


def gather_dp(piece):
    rows, cols = piece.shape
    n = lax.axis_size("dp")
    pieces = [((0,), piece)]
    for group in dp_groups():
        if len(pieces) > 1:
            pieces = [(sum((m for m, _ in pieces), ()), jnp.concatenate([a for _, a in pieces], axis=0))]
        masks, array = pieces[0]
        pieces += [(tuple(m ^ g for m in masks), swap(array, "dp", g)) for g in group]
    pieces += [(tuple(m ^ 1 for m in masks), swap(array, "dp", 1)) for masks, array in pieces]
    me = lax.axis_index("dp")
    if rows % 16 == 0 and all(len(m) == 1 for m, _ in pieces):
        where = jnp.stack([me ^ m[0] for m, _ in pieces]).astype(jnp.int32)
        return assemble([a for _, a in pieces], where)
    order = [m for masks, _ in pieces for m in masks]
    place = [order.index(m) for m in range(n)]
    stacked = jnp.concatenate([a for _, a in pieces], axis=0).reshape(n, rows, cols)
    index = jnp.take(jnp.array(place, jnp.int32), me ^ jnp.arange(n))
    return jnp.take(stacked, index, axis=0).reshape(n * rows, cols)


def assemble_kernel(where, *refs):
    out = refs[-1]
    rows = refs[0].shape[0]
    for s, ref in enumerate(refs[:-1]):
        out[pl.ds(pl.multiple_of(where[s] * rows, rows), rows), :] = ref[...]


def assemble(pieces, where):
    rows, cols = pieces[0].shape
    n = len(pieces)
    block = next(b for b in (1792, 1536, 1024, 896, 768, 512, 256, 128) if cols % b == 0)
    return pl.pallas_call(
        assemble_kernel,
        out_shape=jax.ShapeDtypeStruct((n * rows, cols), pieces[0].dtype),
        grid_spec=pltpu.PrefetchScalarGridSpec(
            num_scalar_prefetch=1,
            grid=(cols // block,),
            in_specs=[pl.BlockSpec((rows, block), lambda i, w: (0, i))] * n,
            out_specs=pl.BlockSpec((n * rows, block), lambda i, w: (0, i)),
        ),
        compiler_params=params(),
        cost_estimate=pl.CostEstimate(flops=0, transcendentals=0, bytes_accessed=4 * n * rows * cols),
        name="assemble",
    )(where, *pieces)


def pick(array, index):
    return lax.dynamic_index_in_dim(array, index, 0, keepdims=False)


def scatter_dp(parts):
    n = lax.axis_size("dp")
    me = lax.axis_index("dp")
    core = me & 1

    def side(c):
        cut = [
            lax.dynamic_index_in_dim(a.reshape(n // 2, 2, a.shape[0] // n, a.shape[1]), c, 1, keepdims=False)
            for a in parts
        ]
        return jnp.concatenate(cut, axis=-1)

    total = side(core).astype(F32) + swap(side(1 - core), "dp", 1).astype(F32)
    for group in reversed(dp_groups()):
        low = group[0]
        count = len(group) + 1
        total = total.reshape(count, -1, *total.shape[1:])
        mine = (me // low) % count
        sent = total.astype(BF)
        terms = [swap(pick(sent, mine ^ (g // low)), "dp", g).astype(F32) for g in group]
        total = pick(total, mine)
        for t in terms:
            total = total + t
    return total.reshape(total.shape[-2:])


def project_kernel(x0, x1, x2, x3, w_ref, b_ref, qt_ref, q_ref, kv_ref, kvt_ref):
    w = w_ref[...]
    keep = lax.broadcasted_iota(jnp.int32, (512, 128), 1) < HD
    for s, x in enumerate((x0, x1, x2, x3)):
        y = dot(x[...], w, 1, 0) + b_ref[0]
        q = jnp.where(keep, y[:, :128].astype(BF).astype(F32) * 0.125, 0.0).astype(BF)
        kv = y[:, 128:].astype(BF)
        q_ref[0, s] = q
        qt_ref[0, s] = q.T
        kv_ref[0, s] = kv
        kvt_ref[0, s] = kv.T


def project(xs, weights, bias):
    heads = bias.shape[0]
    shapes = [(heads, 4, 128, 512), (heads, 4, 512, 128), (heads, 4, 512, 128), (heads, 4, 128, 512)]
    return pl.pallas_call(
        project_kernel,
        grid=(heads,),
        out_shape=[jax.ShapeDtypeStruct(s, BF) for s in shapes],
        in_specs=[whole((512, 768))] * 4
        + [pl.BlockSpec((768, 256), lambda h: (0, h)), pl.BlockSpec((1, 1, 256), lambda h: (h, 0, 0))],
        out_specs=[pl.BlockSpec((1, *s[1:]), lambda h: (h, 0, 0, 0)) for s in shapes],
        compiler_params=params(),
        cost_estimate=pl.CostEstimate(flops=2 * 2048 * 768 * 768, transcendentals=0, bytes_accessed=12 << 20),
        name="project",
    )(*xs, weights, bias)


def masked(scores, count):
    return jnp.where(lax.broadcasted_iota(jnp.int32, scores.shape, 0) < count, scores, NEG)


def attend_kernel(counts, qt_ref, kv_ref, kvt_ref, mt_ref, lse_ref):
    h = pl.program_id(0)
    qt = qt_ref[0, 0]
    scores = [masked(dot(kv_ref[0, j], qt, 1, 0), counts[j]) for j in range(4)]
    peak = functools.reduce(jnp.maximum, [jnp.max(s, axis=0, keepdims=True) for s in scores])
    total = jnp.zeros((1, 512), F32)
    acc = jnp.zeros((128, 512), F32)
    for j in range(4):
        expo = jnp.exp(scores[j] - peak)
        total = total + jnp.sum(expo, axis=0, keepdims=True)
        acc = acc + dot(kvt_ref[0, j], expo.astype(BF), 1, 0)
    mt_ref[pl.ds(pl.multiple_of(h * HD, HD), HD), :] = (acc[HD:] / total).astype(BF)
    lse_ref[0] = peak + jnp.log(total)


def attend(slot, counts, qt, kv, kvt):
    heads = qt.shape[0]
    return pl.pallas_call(
        attend_kernel,
        out_shape=[jax.ShapeDtypeStruct((heads * HD, 512), BF), jax.ShapeDtypeStruct((heads, 1, 512), F32)],
        grid_spec=pltpu.PrefetchScalarGridSpec(
            num_scalar_prefetch=1,
            grid=(heads,),
            in_specs=[
                pl.BlockSpec((1, 1, 128, 512), lambda h, c: (h, slot, 0, 0)),
                pl.BlockSpec((1, 4, 512, 128), lambda h, c: (h, 0, 0, 0)),
                pl.BlockSpec((1, 4, 128, 512), lambda h, c: (h, 0, 0, 0)),
            ],
            out_specs=[
                pl.BlockSpec((heads * HD, 512), lambda h, c: (0, 0)),
                pl.BlockSpec((1, 1, 512), lambda h, c: (h, 0, 0)),
            ],
        ),
        compiler_params=params(),
        cost_estimate=pl.CostEstimate(
            flops=heads * 16 * 2048 * 512 * 64, transcendentals=heads * 2048 * 512, bytes_accessed=4 << 20
        ),
        name="attend",
    )(counts, qt, kv, kvt)


def back_step(counts, qt, q, kv_ref, kvt_ref, dot_rows, lse, dkv_ref, fresh):
    dt = jnp.concatenate([jnp.zeros((HD, 512), BF), dot_rows], axis=0)
    d = dt.T
    probs, grads = [], []
    inner = jnp.zeros((1, 512), F32)
    for j in range(4):
        p = jnp.exp(masked(dot(kv_ref[0, j], qt, 1, 0), counts[j]) - lse)
        g = dot(kv_ref[0, j], dt, 1, 0)
        inner = inner + jnp.sum(p * g, axis=0, keepdims=True)
        probs.append(p)
        grads.append(g)
    dqt = jnp.zeros((128, 512), F32)
    for j in range(4):
        ds = (probs[j] * (grads[j] - inner)).astype(BF)
        dqt = dqt + dot(kvt_ref[0, j], ds, 1, 0)
        dkv = dot(ds, q, 1, 0) + dot(probs[j].astype(BF), d, 1, 0)
        if fresh is None:
            dkv_ref[j] = dkv
        else:
            dkv_ref[j] = dkv_ref[j] + dkv
    return dqt[:HD] * 0.125


def back_own_kernel(counts, qt_ref, q_ref, kv_ref, kvt_ref, dt_ref, lse_ref, dqt_ref, dkv_ref, bias_ref):
    dqt = back_step(
        counts, qt_ref[0, 0], q_ref[0, 0], kv_ref, kvt_ref, dt_ref[...], lse_ref[0], dkv_ref.at[0], None
    )
    dqt_ref[0] = dqt.astype(BF)
    bias_ref[0] = jnp.sum(dqt, axis=1, keepdims=True)


def back_own(counts, qt, q, kv, kvt, dt, lse):
    heads = qt.shape[0]
    return pl.pallas_call(
        back_own_kernel,
        out_shape=[
            jax.ShapeDtypeStruct((heads, HD, 512), BF),
            jax.ShapeDtypeStruct((heads, 4, 512, 128), F32),
            jax.ShapeDtypeStruct((heads, HD, 1), F32),
        ],
        grid_spec=pltpu.PrefetchScalarGridSpec(
            num_scalar_prefetch=1,
            grid=(heads,),
            in_specs=[
                pl.BlockSpec((1, 1, 128, 512), lambda h, c: (h, 0, 0, 0)),
                pl.BlockSpec((1, 1, 512, 128), lambda h, c: (h, 0, 0, 0)),
                pl.BlockSpec((1, 4, 512, 128), lambda h, c: (h, 0, 0, 0)),
                pl.BlockSpec((1, 4, 128, 512), lambda h, c: (h, 0, 0, 0)),
                pl.BlockSpec((HD, 512), lambda h, c: (h, 0)),
                pl.BlockSpec((1, 1, 512), lambda h, c: (h, 0, 0)),
            ],
            out_specs=[
                pl.BlockSpec((1, HD, 512), lambda h, c: (h, 0, 0)),
                pl.BlockSpec((1, 4, 512, 128), lambda h, c: (h, 0, 0, 0)),
                pl.BlockSpec((1, HD, 1), lambda h, c: (h, 0, 0)),
            ],
        ),
        compiler_params=params(),
        cost_estimate=pl.CostEstimate(
            flops=heads * 40 * 2048 * 512 * 64, transcendentals=heads * 2048 * 512, bytes_accessed=8 << 20
        ),
        name="back_own",
    )(counts, qt, q, kv, kvt, dt, lse)


def back_head_kernel(
    counts, qt_ref, q_ref, kv_ref, kvt_ref, d1, d2, d3, l1, l2, l3, dq0_ref, dkv_ref, b_ref, x0, x1, x2, x3,
    p0, p1, p2, p3, dw_ref, qb_ref, vb_ref, acc, dqs,
):
    s = pl.program_id(0)

    @pl.when(s == 0)
    def _():
        acc[...] = dkv_ref[0]
        dqs[0] = dq0_ref[0]
        qb_ref[...] = b_ref[0]

    rows = jnp.where(s == 0, d1[...], jnp.where(s == 1, d2[...], d3[...]))
    lse = jnp.where(s == 0, l1[0], jnp.where(s == 1, l2[0], l3[0]))
    dqt = back_step(counts, qt_ref[0, 0], q_ref[0, 0], kv_ref, kvt_ref, rows, lse, acc, True)
    dqs[s + 1] = dqt.astype(BF)
    qb_ref[...] += jnp.sum(dqt, axis=1, keepdims=True)

    @pl.when(s == 2)
    def _():
        dwt = jnp.zeros((3 * HD, 768), F32)
        vsum = jnp.zeros((1, 128), F32)
        for j, (packet, x) in enumerate(((p0, x0), (p1, x1), (p2, x2), (p3, x3))):
            part = acc[j]
            vsum = vsum + jnp.sum(part, axis=0, keepdims=True)
            both = jnp.concatenate([dqs[j], part.astype(BF).T], axis=0)
            packet[...] = both
            dwt = dwt + dot(both, x[...], 1, 0)
        vb_ref[...] = vsum
        dw_ref[...] = dwt.T.astype(BF)


def back_head(h, counts, qt, q, kv, kvt, dts, lses, dq0, dkv, bias0, xs):
    spec = pl.BlockSpec
    return pl.pallas_call(
        back_head_kernel,
        out_shape=[jax.ShapeDtypeStruct((3 * HD, 512), BF)] * 4
        + [
            jax.ShapeDtypeStruct((768, 3 * HD), BF),
            jax.ShapeDtypeStruct((HD, 1), F32),
            jax.ShapeDtypeStruct((1, 128), F32),
        ],
        grid_spec=pltpu.PrefetchScalarGridSpec(
            num_scalar_prefetch=1,
            grid=(3,),
            in_specs=[
                spec((1, 1, 128, 512), lambda s, c: (h, s + 1, 0, 0)),
                spec((1, 1, 512, 128), lambda s, c: (h, s + 1, 0, 0)),
                spec((1, 4, 512, 128), lambda s, c: (h, 0, 0, 0)),
                spec((1, 4, 128, 512), lambda s, c: (h, 0, 0, 0)),
            ]
            + [spec((HD, 512), lambda s, c: (h, 0))] * 3
            + [spec((1, 1, 512), lambda s, c: (h, 0, 0))] * 3
            + [
                spec((1, HD, 512), lambda s, c: (h, 0, 0)),
                spec((1, 4, 512, 128), lambda s, c: (h, 0, 0, 0)),
                spec((1, HD, 1), lambda s, c: (h, 0, 0)),
            ]
            + [spec((512, 768), lambda s, c: (0, 0))] * 4,
            out_specs=[spec((3 * HD, 512), lambda s, c: (0, 0))] * 4
            + [
                spec((768, 3 * HD), lambda s, c: (0, 0)),
                spec((HD, 1), lambda s, c: (0, 0)),
                spec((1, 128), lambda s, c: (0, 0)),
            ],
            scratch_shapes=[pltpu.VMEM((4, 512, 128), F32), pltpu.VMEM((4, HD, 512), BF)],
        ),
        compiler_params=params(),
        cost_estimate=pl.CostEstimate(
            flops=3 * 40 * 2048 * 512 * 64, transcendentals=3 * 2048 * 512, bytes_accessed=8 << 20
        ),
        name="back_head",
    )(counts, qt, q, kv, kvt, *dts, *lses, dq0, dkv, bias0, *xs)


def row_mean(v):
    return jnp.mean(v, axis=1, keepdims=True)


def norm(rows):
    center = rows - row_mean(rows)
    spread = lax.rsqrt(row_mean(center * center) + EPS)
    return center * spread, spread


def norm_back(grad, normed, spread, gain):
    scaled = grad * gain
    return spread * (scaled - row_mean(scaled) - normed * row_mean(scaled * normed))


def middle_kernel(
    count, m0, m1, m2, m3, x_ref, cot_ref, wo_ref, wf_ref, vec_ref, ib_ref,
    out_ref, g1_ref, d0, d1, d2, d3, dwo_ref, dwf_ref, dvec_ref, dib_ref,
    n1_ref, s1_ref, hid_ref, hidb_ref, hidt_ref, acc_ref, gp_ref, act_ref, gs_ref, gsb_ref, gst_ref,
):
    step = pl.program_id(0)
    vec = lambda i: vec_ref[pl.ds(i, 1), :]
    mixed = (m0, m1, m2, m3)

    @pl.when(step == 0)
    def _():
        rows = x_ref[...].astype(F32) + vec(0)
        for k in range(4):
            rows = rows + dot(mixed[k][...], wo_ref[:, k * 256 : k * 256 + 192], 0, 1)
        n1, s1 = norm(rows)
        hidden = n1 * vec(1) + vec(2)
        n1_ref[...] = n1
        s1_ref[...] = s1
        hid_ref[...] = hidden
        low = hidden.astype(BF)
        hidb_ref[...] = low
        hidt_ref[...] = low.T
        acc_ref[...] = hidden + vec(3)

    @pl.when(step < 4)
    def _():
        u = dot(hidb_ref[...], wf_ref[:, :768], 1, 0) + ib_ref[pl.ds(step, 1), :]
        cdf = 0.5 + 0.5 * lax.erf(u * math.sqrt(0.5))
        act = (u * cdf).astype(BF)
        gp_ref[step] = cdf + u * jnp.exp(-0.5 * u * u) * (1.0 / math.sqrt(2.0 * math.pi))
        act_ref[step] = act
        acc_ref[...] += dot(act, wf_ref[:, 768:], 1, 1)

    @pl.when(step == 3)
    def _():
        valid = (lax.broadcasted_iota(jnp.int32, (512, 1), 0) < count[0]).astype(F32)
        n2, s2 = norm(acc_ref[...])
        out_ref[...] = (valid * (n2 * vec(4) + vec(5))).astype(BF)
        g2 = cot_ref[...].astype(F32) * valid
        gs = norm_back(g2, n2, s2, vec(4))
        gs_ref[...] = gs
        low = gs.astype(BF)
        gsb_ref[...] = low
        gst_ref[...] = low.T
        dvec_ref[pl.ds(3, 1), :] = jnp.sum(gs, axis=0, keepdims=True)
        dvec_ref[pl.ds(4, 1), :] = jnp.sum(g2 * n2, axis=0, keepdims=True)
        dvec_ref[pl.ds(5, 1), :] = jnp.sum(g2, axis=0, keepdims=True)
        acc_ref[...] = gs

    @pl.when(step >= 4)
    def _():
        k = step - 4
        gi = dot(gsb_ref[...], wf_ref[:, 768:], 1, 0) * gp_ref[k]
        dib_ref[pl.ds(k, 1), :] = jnp.sum(gi, axis=0, keepdims=True)
        low = gi.astype(BF)
        acc_ref[...] += dot(low, wf_ref[:, :768], 1, 1)
        dwf_ref[:, :768] = dot(hidt_ref[...], low, 1, 0).astype(BF)
        dwf_ref[:, 768:] = dot(gst_ref[...], act_ref[k], 1, 0).astype(BF)

    @pl.when(step == 7)
    def _():
        gh = acc_ref[...]
        n1 = n1_ref[...]
        g1 = norm_back(gh, n1, s1_ref[...], vec(1))
        g1_ref[...] = g1
        dvec_ref[pl.ds(0, 1), :] = jnp.sum(g1, axis=0, keepdims=True)
        dvec_ref[pl.ds(1, 1), :] = jnp.sum(gh * n1, axis=0, keepdims=True)
        dvec_ref[pl.ds(2, 1), :] = jnp.sum(gh, axis=0, keepdims=True)
        dvec_ref[pl.ds(6, 2), :] = jnp.zeros((2, 768), F32)
        low = g1.astype(BF)
        lowt = low.T
        for k, d in enumerate((d0, d1, d2, d3)):
            d[...] = dot(wo_ref[:, k * 256 : k * 256 + 192], lowt, 0, 0).astype(BF)
            dwo_ref[:, k * 256 : k * 256 + 192] = dot(lowt, mixed[k][...], 1, 1).astype(BF)
            dwo_ref[:, k * 256 + 192 : k * 256 + 256] = jnp.zeros((768, 64), BF)


def middle(count, mixed, x, cot, wo, wf, vec, ib):
    spec = pl.BlockSpec
    fixed = lambda shape: spec(shape, lambda i, c: (0,) * len(shape))
    once = lambda shape: spec(shape, lambda i, c: (0,) * len(shape), pipeline_mode=pl.Buffered(1))
    shape = jax.ShapeDtypeStruct
    return pl.pallas_call(
        middle_kernel,
        out_shape=[shape((512, 768), BF), shape((512, 768), F32)]
        + [shape((192, 512), BF)] * 4
        + [shape((768, 1024), BF), shape((768, 6144), BF), shape((8, 768), F32), shape((4, 768), F32)],
        grid_spec=pltpu.PrefetchScalarGridSpec(
            num_scalar_prefetch=1,
            grid=(8,),
            in_specs=[fixed((192, 512))] * 4
            + [fixed((512, 768)), fixed((512, 768)), fixed((768, 1024))]
            + [spec((768, 1536), lambda i, c: (0, lax.rem(i, 4))), fixed((8, 768)), fixed((4, 768))],
            out_specs=[fixed((512, 768)), fixed((512, 768))]
            + [fixed((192, 512))] * 4
            + [fixed((768, 1024))]
            + [spec((768, 1536), lambda i, c: (0, jnp.maximum(i - 4, 0))), fixed((8, 768)), fixed((4, 768))],
            scratch_shapes=[
                pltpu.VMEM((512, 768), F32),
                pltpu.VMEM((512, 1), F32),
                pltpu.VMEM((512, 768), F32),
                pltpu.VMEM((512, 768), BF),
                pltpu.VMEM((768, 512), BF),
                pltpu.VMEM((512, 768), F32),
                pltpu.VMEM((4, 512, 768), F32),
                pltpu.VMEM((4, 512, 768), BF),
                pltpu.VMEM((512, 768), F32),
                pltpu.VMEM((512, 768), BF),
                pltpu.VMEM((768, 512), BF),
            ],
        ),
        compiler_params=params(),
        cost_estimate=pl.CostEstimate(
            flops=6 * 2 * 512 * 768 * 3072 + 3 * 2 * 512 * 768 * 768,
            transcendentals=2 * 512 * 3072,
            bytes_accessed=40 << 20,
        ),
        name="middle",
    )(count, *mixed, x, cot, wo, wf, vec, ib)


def input_grad_kernel(g1_ref, w_ref, *refs):
    packets, out, acc = refs[:12], refs[12], refs[13]
    total = jnp.zeros((768, 512), F32)
    for k in range(4):
        for h in range(3):
            p = packets[h * 4 + k]
            lane = (k * 3 + h) * 256
            dq = jnp.concatenate([p[:HD], jnp.zeros((HD, 512), BF)], axis=0)
            total = total + dot(w_ref[:, lane : lane + 128], dq, 1, 0)
            total = total + dot(w_ref[:, lane + 128 : lane + 256], p[HD:], 1, 0)
    acc[...] = total
    out[...] = g1_ref[...] + acc[...].T


def input_grad(g1, weights, packets):
    return pl.pallas_call(
        input_grad_kernel,
        grid=(1,),
        out_shape=jax.ShapeDtypeStruct((512, 768), F32),
        in_specs=[whole((512, 768)), whole((768, 3072))] + [whole((192, 512))] * 12,
        out_specs=whole((512, 768)),
        scratch_shapes=[pltpu.VMEM((768, 512), F32)],
        compiler_params=params(),
        cost_estimate=pl.CostEstimate(flops=2 * 512 * 768 * 3072, transcendentals=0, bytes_accessed=10 << 20),
        name="input_grad",
    )(g1, weights, *packets)


def body(
    tokens, cotangent, lengths, query_weight, key_weight, value_weight, query_bias, value_bias, output_weight,
    output_bias, first_gain, first_shift, inner_weight, inner_bias, outer_weight, outer_bias, second_gain, second_shift,
):
    n = lax.axis_size("dp")
    rows = query_weight.shape[0]
    heads = query_weight.shape[1] // HD
    z = lax.axis_index("tensor")
    slots = jnp.arange(4) ^ z
    counts = jnp.clip(lengths[0] - slots * 512, 0, 512).astype(jnp.int32)

    by_head = lambda w: w.reshape(rows, heads, HD)
    wide = jnp.stack(
        [by_head(query_weight), by_head(output_weight), by_head(key_weight), by_head(value_weight)], axis=2
    ).reshape(rows, heads * 256)
    small = jnp.stack([output_bias, first_gain, first_shift, outer_bias, second_gain, second_shift], axis=1)
    few = query_bias.shape[0]
    biases = jnp.pad(jnp.concatenate([query_bias, value_bias], axis=1), ((0, rows - few), (0, 0)))
    tile = jnp.concatenate([small, biases, jnp.zeros((rows, 128 - 6 - 2 * heads), BF)], axis=1)
    near = gather_dp(jnp.concatenate([wide, tile], axis=1))

    xs = gather_tensor(tokens)

    extra = jnp.pad(inner_bias, ((0, rows - few), (0, 64 - inner_bias.shape[1])))
    front = jnp.concatenate([inner_weight, outer_weight, output_weight, extra], axis=1)
    front = gather_tensor(front)
    front = gather_dp(jnp.concatenate([f[:, :1536] for f in front] + [f[:, 1536:] for f in front], axis=1))

    tile = near[:, heads * 256 :].astype(F32)
    vec = jnp.pad(tile[:, :6].T, ((0, 2), (0, 0)))
    pair = tile.reshape(n, rows, 128)[:, :few, 6 : 6 + 2 * heads].reshape(HD, 2, heads)
    bias = jnp.concatenate([pair[:, 0].T, jnp.zeros((heads, 2 * HD), F32), pair[:, 1].T], axis=1)[:, None, :]
    qt, q, kv, kvt = project(xs, near[:, : heads * 256], bias)

    mixed, lses = [None] * 4, [None] * 4
    for s in (3, 2, 1, 0):
        mixed[s], lses[s] = attend(s, counts, qt, kv, kvt)
    mixed = [mixed[0]] + [swap(mixed[m], "tensor", m) for m in (1, 2, 3)]

    wf, wo = front[:, :6144], front[:, 6144:]
    units = inner_bias.shape[1]
    ib = wo.reshape(n, rows, 4, 256)[:, :few, :, 192 : 192 + units].astype(F32)
    ib = ib.transpose(2, 3, 0, 1).reshape(4, units * HD)
    out, g1, d0, d1, d2, d3, dwo, dwf, dvec, dib = middle(counts[:1], mixed, tokens, cotangent, wo, wf, vec, ib)

    ibg = dib.reshape(4, units, n, few).transpose(2, 3, 0, 1)
    ibg = jnp.pad(ibg, ((0, 0), (0, rows - few), (0, 0), (0, 0))).reshape(n * rows, 4, units)
    cols = jnp.broadcast_to(dvec[:6].T[:, None, :], (n * rows, 4, 6))
    rest = jnp.concatenate([cols, ibg, jnp.zeros((n * rows, 4, 64 - 6 - units), F32)], axis=2).astype(BF)
    tail = jnp.concatenate([dwo.reshape(-1, 4, 256)[:, :, :192], rest], axis=2).reshape(n * rows, 1024)
    part = scatter_dp([dwf, tail]).astype(BF)
    parts = [
        jnp.concatenate([part[:, k * 1536 : k * 1536 + 1536], part[:, 6144 + k * 256 : 6400 + k * 256]], axis=1)
        for k in range(4)
    ]
    parts = [parts[0]] + [swap(parts[m], "tensor", m) for m in (1, 2, 3)]
    parts = [p.astype(F32) for p in parts]
    front_grad = (parts[0] + parts[1]) + (parts[2] + parts[3])

    dts = [d0] + [swap(d, "tensor", m) for m, d in ((1, d1), (2, d2), (3, d3))]
    dq0, dkv, bias0 = back_own(counts, qt, q, kv, kvt, dts[0], lses[0])
    packets, dws, qbs, vbs = [], [], [], []
    for h in range(heads):
        *ps, dw, qb, vb = back_head(h, counts, qt, q, kv, kvt, dts[1:], lses[1:], dq0, dkv, bias0, xs)
        packets += [ps[0]] + [swap(ps[m], "tensor", m) for m in (1, 2, 3)]
        dws.append(dw)
        qbs.append(qb[:, 0])
        vbs.append(vb[0, HD:])

    wide, _ = lax.optimization_barrier((wide, g1))
    full = gather_dp(jnp.concatenate(gather_tensor(wide), axis=1))
    tokens_grad = input_grad(g1, full, packets)

    bg = jnp.stack(qbs + vbs, axis=1).astype(BF).reshape(n, few, 2 * heads)
    bg = jnp.pad(bg, ((0, 0), (0, rows - few), (0, 64 - 2 * heads))).reshape(n * rows, 64)
    own = scatter_dp(dws + [bg])
    head = lambda i: jnp.concatenate([own[:, h * 192 + i * 64 : h * 192 + i * 64 + 64] for h in range(heads)], axis=1)
    vectors = front_grad[:, 1536 + 192 :]
    bgs = own[:few, heads * 192 :]
    return (
        out,
        tokens_grad,
        head(0),
        head(1),
        head(2),
        bgs[:, :heads],
        bgs[:, heads : 2 * heads],
        front_grad[:, 1536:1728],
        vectors[:, 0],
        vectors[:, 1],
        vectors[:, 2],
        front_grad[:, :768],
        vectors[:few, 6 : 6 + units],
        front_grad[:, 768:1536],
        vectors[:, 3],
        vectors[:, 4],
        vectors[:, 5],
    )


def solution(mesh):
    table, vector, token = P("dp", "tensor"), P("dp"), P(("dp", "tensor"), None)
    return jax.shard_map(
        body,
        mesh=mesh,
        in_specs=(
            token, token, vector, table, table, table, table, table, table,
            vector, vector, vector, table, table, table, vector, vector, vector,
        ),
        out_specs=(
            token, token, table, table, table, table, table, table,
            vector, vector, vector, table, table, table, vector, vector, vector,
        ),
        check_vma=False,
    )
```

```python
import functools
import math

import jax
import jax.numpy as jnp
from jax import lax
from jax.experimental import pallas as pl
from jax.experimental.pallas import tpu as pltpu
from jax.sharding import PartitionSpec as P

HD = 64
SLOT_LEN = 2048
EPS = 1e-05
NEG = -1e30
BF = jnp.bfloat16
F32 = jnp.float32
VMEM_LIMIT = 60 * 1024 * 1024
LIGHT = pl.CostEstimate(flops=1, transcendentals=0, bytes_accessed=1)


def dot(a, b, ca, cb):
    return lax.dot_general(a, b, (((ca,), (cb,)), ((), ())), preferred_element_type=F32)


def whole(shape):
    return pl.BlockSpec(shape, lambda *_: (0,) * len(shape))


def params():
    return pltpu.CompilerParams(vmem_limit_bytes=VMEM_LIMIT)


def swap(x, axis, mask):
    n = lax.axis_size(axis)
    return lax.ppermute(x, axis, [(i, i ^ mask) for i in range(n)])


def dp_groups():
    n, bit, groups = lax.axis_size("dp"), 2, []
    while bit < n:
        if bit * 2 < n:
            groups.append((bit, bit * 2, bit * 3))
            bit *= 4
        else:
            groups.append((bit,))
            bit *= 2
    return groups


def stage(*values):
    return lax.optimization_barrier(values)


def shift(x, by):
    n = lax.axis_size("tensor")
    return lax.ppermute(x, "tensor", [(i, i + by) for i in range(n) if 0 <= i + by < n])


def by_slot(up, down, k):
    z = lax.axis_index("tensor")
    odd, high = z % 2 == 1, z >= 2
    if k == 0:
        return up[0]
    if k == 1:
        return jnp.where(odd, up[1], down[1])
    if k == 2:
        return jnp.where(high, up[2], down[2])
    return jnp.where(odd, jnp.where(high, up[3], down[1]), jnp.where(high, up[1], down[3]))


def exchange(blocks):
    return lax.all_to_all(blocks, "tensor", 0, 0)


def aligned(rows):
    return rows % 16 == 0 and lax.axis_size("dp") == 8


def gather_all(piece):
    n, t = lax.axis_size("dp"), lax.axis_size("tensor")
    rows, cols = piece.shape
    blocks = lax.all_gather(piece, ("dp", "tensor")).reshape(n, t, rows, cols)
    if aligned(rows):
        return blocks
    return blocks.transpose(1, 0, 2, 3).reshape(1, t, n * rows, cols)


def gather_rows(piece):
    rows, cols = piece.shape
    n = lax.axis_size("dp")
    me = lax.axis_index("dp")
    pieces = [((0,), piece)]
    for group in dp_groups():
        if len(pieces) > 1:
            pieces = [(sum((m for m, _ in pieces), ()), jnp.concatenate([a for _, a in pieces], axis=0))]
        masks, array = pieces[0]
        pieces += [(tuple(m ^ g for m in masks), swap(array, "dp", g)) for g in group]
    pieces += [(tuple(m ^ 1 for m in masks), swap(array, "dp", 1)) for masks, array in pieces]
    order = [m for masks, _ in pieces for m in masks]
    place = [order.index(m) for m in range(n)]
    stacked = jnp.concatenate([a for _, a in pieces], axis=0).reshape(n, rows, cols)
    index = jnp.take(jnp.array(place, jnp.int32), me ^ jnp.arange(n))
    return jnp.take(stacked, index, axis=0).reshape(n * rows, cols)


def put(where, refs, out):
    if len(refs) == 1:
        out[...] = refs[0][...]
        return
    count = out.shape[0] // refs[0].shape[0]
    each = (where.shape[0] if hasattr(where, "shape") else len(where)) // count
    rows = refs[0].shape[0] // each
    for s, ref in enumerate(refs):
        for b in range(each):
            out[pl.ds(pl.multiple_of(where[each * s + b], rows), rows), :] = ref[b * rows : (b + 1) * rows]


def assemble_kernel(where, *refs):
    put(where, refs[:-1], refs[-1])


def assemble(pieces, where, block, at):
    rows, n = pieces[0].shape[0], len(pieces)
    return pl.pallas_call(
        assemble_kernel,
        out_shape=jax.ShapeDtypeStruct((n * rows, block), pieces[0].dtype),
        grid_spec=pltpu.PrefetchScalarGridSpec(
            num_scalar_prefetch=1,
            grid=(1,),
            in_specs=[pl.BlockSpec((rows, block), lambda i, w: (0, at))] * n,
            out_specs=pl.BlockSpec((n * rows, block), lambda i, w: (0, 0)),
        ),
        compiler_params=params(),
        cost_estimate=LIGHT,
        name="assemble",
    )(where, *pieces)


def split_rows(place, value, keep, send, lane):
    lanes = slice(lane, lane + value.shape[1])
    if send is None:
        keep[:, lanes] = value
        return
    rows = keep.shape[1]
    for j in range(4):
        at = jnp.bitwise_xor(j, place[1])
        even, odd = value[2 * j * rows : (2 * j + 1) * rows], value[(2 * j + 1) * rows : (2 * j + 2) * rows]
        keep[at, :, lanes] = jnp.where(place[0] == 0, even, odd)
        send[at, :, lanes] = jnp.where(place[0] == 0, odd, even)


def add_kernel(groups, *refs):
    outs = refs[len(refs) - len(groups) :]
    for out, terms in zip(outs, groups, strict=True):
        total = refs[terms[0]][...].astype(F32)
        for t in terms[1:]:
            total = total + refs[t][...].astype(F32)
        out[...] = total.reshape(out.shape).astype(out.dtype)


def add(terms, outs):
    lanes = outs[0][1]
    block = 1792
    specs = []
    for array, lead, start in terms:
        rows = array.shape[-2]
        if lead is None:
            specs.append(pl.BlockSpec((rows, block), lambda i, s=start // block: (0, i + s)))
        else:
            specs.append(pl.BlockSpec((1, rows, block), lambda i, m=lead, s=start // block: (m, 0, i + s)))
    rows = terms[0][0].shape[-2]
    return pl.pallas_call(
        functools.partial(add_kernel, [numbers for numbers, _, _ in outs]),
        grid=(lanes // block,),
        out_shape=[jax.ShapeDtypeStruct((rows, lanes), d) for _, _, d in outs],
        in_specs=specs,
        out_specs=[pl.BlockSpec((rows, block), lambda i: (0, i))] * len(outs),
        compiler_params=params(),
        cost_estimate=LIGHT,
        name="add",
    )(*[a for a, _, _ in terms])


def sum_rows(array):
    n = lax.axis_size("dp")
    me = lax.axis_index("dp")
    halves = array.reshape(n // 2, 2, array.shape[0] // n, array.shape[1])
    side = lambda c: lax.dynamic_index_in_dim(halves, c, 1, keepdims=False)
    total = side(me & 1).astype(F32) + swap(side(1 - (me & 1)), "dp", 1).astype(F32)
    for group in reversed(dp_groups()):
        count = len(group) + 1
        total = total.reshape(count, -1, *total.shape[1:])
        mine = (me // group[0]) % count
        sent = total.astype(BF)
        terms = [swap(pick(sent, mine ^ (g // group[0])), "dp", g).astype(F32) for g in group]
        total = pick(total, mine)
        for t in terms:
            total = total + t
    return total.reshape(total.shape[-2:])


def pick(array, index):
    return lax.dynamic_index_in_dim(array, index, 0, keepdims=False)


def split_shapes(aligned_rows, rows, cols):
    shape = jax.ShapeDtypeStruct
    return [shape((4, rows, cols), BF)] * 2 if aligned_rows else [shape((768, cols), BF)]


def spread(rows, few):
    i = lax.broadcasted_iota(jnp.int32, (768, HD), 1)
    r = lax.broadcasted_iota(jnp.int32, (768, HD), 0)
    return (r == (i // few) * rows + i % few).astype(F32).astype(BF)


def project_kernel(where, x_ref, b_ref, *refs):
    pieces, (qt_ref, q_ref, kv_ref, kvt_ref, w) = refs[:-5], refs[-5:]
    put(where, pieces, w)
    y = dot(x_ref[...], w[...], 1, 0) + b_ref[0]
    keep = lax.broadcasted_iota(jnp.int32, (512, 128), 1) < HD
    q = jnp.where(keep, y[:, :128].astype(BF).astype(F32) * 0.125, 0.0).astype(BF)
    kv = y[:, 128:].astype(BF)
    q_ref[0] = q
    qt_ref[0] = q.T
    kv_ref[0] = kv
    kvt_ref[0] = kv.T


def project(x, near, bias):
    pieces, where = near
    heads, rows = bias.shape[0], pieces[0].shape[0]
    shapes = [(heads, 128, 512), (heads, 512, 128), (heads, 512, 128), (heads, 128, 512)]
    return pl.pallas_call(
        project_kernel,
        out_shape=[jax.ShapeDtypeStruct(s, BF) for s in shapes],
        grid_spec=pltpu.PrefetchScalarGridSpec(
            num_scalar_prefetch=1,
            grid=(heads,),
            in_specs=[whole((512, 768)), pl.BlockSpec((1, 1, 256), lambda h, w: (h, 0, 0))]
            + [pl.BlockSpec((rows, 256), lambda h, w: (0, h))] * len(pieces),
            out_specs=[pl.BlockSpec((1, *s[1:]), lambda h, w: (h, 0, 0)) for s in shapes],
            scratch_shapes=[pltpu.VMEM((768, 256), BF)],
        ),
        compiler_params=params(),
        cost_estimate=LIGHT,
        name="project",
    )(where, x, bias, *pieces)


def masked(scores, count):
    return jnp.where(lax.broadcasted_iota(jnp.int32, scores.shape, 0) < count, scores, NEG)


def attend_kernel(counts, qt_ref, k0, k1, k2, k3, t0, t1, t2, t3, mt_ref, lse_ref):
    h = pl.program_id(0)
    qt = qt_ref[0]
    kvt = (t0, t1, t2, t3)
    scores = [masked(dot(k[0], qt, 1, 0), counts[j]) for j, k in enumerate((k0, k1, k2, k3))]
    peak = functools.reduce(jnp.maximum, [jnp.max(s, axis=0, keepdims=True) for s in scores])
    total = jnp.zeros((1, 512), F32)
    acc = jnp.zeros((128, 512), F32)
    for j in range(4):
        expo = jnp.exp(scores[j] - peak)
        total = total + jnp.sum(expo, axis=0, keepdims=True)
        acc = acc + dot(kvt[j][0], expo.astype(BF), 1, 0)
    mt_ref[pl.ds(pl.multiple_of(h * HD, HD), HD), :] = (acc[HD:] / total).astype(BF)
    lse_ref[0] = peak + jnp.log(total)


def attend(counts, qt, kv, kvt):
    heads = qt.shape[0]
    return pl.pallas_call(
        attend_kernel,
        out_shape=[jax.ShapeDtypeStruct((heads * HD, 512), BF), jax.ShapeDtypeStruct((heads, 1, 512), F32)],
        grid_spec=pltpu.PrefetchScalarGridSpec(
            num_scalar_prefetch=1,
            grid=(heads,),
            in_specs=[pl.BlockSpec((1, 128, 512), lambda h, c: (h, 0, 0))]
            + [pl.BlockSpec((1, 512, 128), lambda h, c: (h, 0, 0))] * 4
            + [pl.BlockSpec((1, 128, 512), lambda h, c: (h, 0, 0))] * 4,
            out_specs=[
                pl.BlockSpec((heads * HD, 512), lambda h, c: (0, 0)),
                pl.BlockSpec((1, 1, 512), lambda h, c: (h, 0, 0)),
            ],
        ),
        compiler_params=params(),
        cost_estimate=LIGHT,
        name="attend",
    )(counts, qt, *kv, *kvt)


def back_step(counts, qt, q, kv, kvt, dot_rows, lse, dkv_ref, fresh):
    dt = jnp.concatenate([jnp.zeros((HD, 512), BF), dot_rows], axis=0)
    d = dt.T
    probs, grads = [], []
    inner = jnp.zeros((1, 512), F32)
    for j in range(4):
        p = jnp.exp(masked(dot(kv[j][0], qt, 1, 0), counts[j]) - lse)
        g = dot(kv[j][0], dt, 1, 0)
        inner = inner + jnp.sum(p * g, axis=0, keepdims=True)
        probs.append(p)
        grads.append(g)
    dqt = jnp.zeros((128, 512), F32)
    for j in range(4):
        ds = (probs[j] * (grads[j] - inner)).astype(BF)
        dqt = dqt + dot(kvt[j][0], ds, 1, 0)
        dkv = dot(ds, q, 1, 0) + dot(probs[j].astype(BF), d, 1, 0)
        if fresh is None:
            dkv_ref[j] = dkv
        else:
            dkv_ref[j] = dkv_ref[j] + dkv
    return dqt[:HD] * 0.125


def back_own_kernel(counts, qt_ref, q_ref, *refs):
    kv, kvt, (dt_ref, lse_ref, dqt_ref, dkv_ref, bias_ref) = refs[:4], refs[4:8], refs[8:]
    dqt = back_step(counts, qt_ref[0], q_ref[0], kv, kvt, dt_ref[0], lse_ref[0], dkv_ref.at[0], None)
    dqt_ref[0] = dqt.astype(BF)
    bias_ref[0] = jnp.sum(dqt, axis=1, keepdims=True)


def back_own(counts, qt, q, kv, kvt, dt, lse):
    heads = qt.shape[0]
    tall, flat = pl.BlockSpec((1, 512, 128), lambda h, c: (h, 0, 0)), pl.BlockSpec((1, 128, 512), lambda h, c: (h, 0, 0))
    return pl.pallas_call(
        back_own_kernel,
        out_shape=[
            jax.ShapeDtypeStruct((heads, HD, 512), BF),
            jax.ShapeDtypeStruct((heads, 4, 512, 128), F32),
            jax.ShapeDtypeStruct((heads, HD, 1), F32),
        ],
        grid_spec=pltpu.PrefetchScalarGridSpec(
            num_scalar_prefetch=1,
            grid=(heads,),
            in_specs=[flat, tall]
            + [tall] * 4
            + [flat] * 4
            + [
                pl.BlockSpec((1, HD, 512), lambda h, c: (c[6], h, 0)),
                pl.BlockSpec((1, 1, 512), lambda h, c: (h, 0, 0)),
            ],
            out_specs=[
                pl.BlockSpec((1, HD, 512), lambda h, c: (h, 0, 0)),
                pl.BlockSpec((1, 4, 512, 128), lambda h, c: (h, 0, 0, 0)),
                pl.BlockSpec((1, HD, 1), lambda h, c: (h, 0, 0)),
            ],
        ),
        compiler_params=params(),
        cost_estimate=LIGHT,
        name="back_own",
    )(counts, qt, q, *kv, *kvt, dt, lse)


def back_head_kernel(few, apart, sc, *refs):
    qts, qs, kv, kvt = refs[:3], refs[3:6], refs[6:10], refs[10:14]
    ds, ls, (dq0_ref, dkv_ref, b_ref), xs = refs[14:17], refs[17:20], refs[20:23], refs[23:27]
    packet, outs, (acc, dqs, qb) = refs[27], refs[28:-3], refs[-3:]
    s = pl.program_id(0)

    @pl.when(s == 0)
    def _():
        acc[...] = dkv_ref[0]
        dqs[0] = dq0_ref[0]
        qb[...] = b_ref[0]

    choose = lambda a: jnp.where(s == 0, a[0], jnp.where(s == 1, a[1], a[2]))
    rows = choose([d[0] for d in ds])
    lse = choose([v[0] for v in ls])
    qt, q = choose([v[0] for v in qts]), choose([v[0] for v in qs])
    dqt = back_step(sc, qt, q, kv, kvt, rows, lse, acc, True)
    dqs[s + 1] = dqt.astype(BF)
    qb[...] += jnp.sum(dqt, axis=1, keepdims=True)

    @pl.when(s == 2)
    def _():
        dwt = jnp.zeros((256, 768), F32)
        vsum = jnp.zeros((1, 128), F32)
        for j in range(4):
            part = acc[j]
            vsum = vsum + jnp.sum(part, axis=0, keepdims=True)
            both = jnp.concatenate([dqs[j], part.astype(BF).T], axis=0)
            packet[jnp.bitwise_xor(sc[6], j)] = both
            both = jnp.concatenate([both, jnp.zeros((HD, 512), BF)], axis=0)
            dwt = dwt + dot(both, xs[j][...], 1, 0)
        lane = lax.broadcasted_iota(jnp.int32, (HD, 256), 1)
        vcol = jnp.broadcast_to(vsum, (128, 128)).T[HD:, :1]
        sums = jnp.where(lane == 192, qb[...], jnp.where(lane == 193, vcol, 0.0)).astype(BF)
        rows = 768 * few // HD
        dw = dwt.T + dot(spread(rows, few), sums, 1, 0)
        split_rows((sc[4], sc[5]), dw.astype(BF), outs[0], outs[1] if apart else None, 0)


def back_head(h, sc, qt, q, kv, kvt, dts, lses, dq0, dkv, bias0, xs, few):
    spec = pl.BlockSpec
    rows = 768 * few // HD
    apart = aligned(rows)
    tall, flat = spec((1, 512, 128), lambda s, c: (h, 0, 0)), spec((1, 128, 512), lambda s, c: (h, 0, 0))
    splits = split_shapes(apart, rows, 256)
    return pl.pallas_call(
        functools.partial(back_head_kernel, few, apart),
        out_shape=[jax.ShapeDtypeStruct((4, 3 * HD, 512), BF)] + splits,
        grid_spec=pltpu.PrefetchScalarGridSpec(
            num_scalar_prefetch=1,
            grid=(3,),
            in_specs=[flat] * 3
            + [tall] * 3
            + [tall] * 4
            + [flat] * 4
            + [spec((1, HD, 512), lambda s, c, j=j: (jnp.bitwise_xor(c[6], j), h, 0)) for j in (1, 2, 3)]
            + [spec((1, 1, 512), lambda s, c: (h, 0, 0))] * 3
            + [
                spec((1, HD, 512), lambda s, c: (h, 0, 0)),
                spec((1, 4, 512, 128), lambda s, c: (h, 0, 0, 0)),
                spec((1, HD, 1), lambda s, c: (h, 0, 0)),
            ]
            + [spec((512, 768), lambda s, c: (0, 0))] * 4,
            out_specs=[spec((4, 3 * HD, 512), lambda s, c: (0, 0, 0))]
            + [spec(v.shape, lambda s, c, d=len(v.shape): (0,) * d) for v in splits],
            scratch_shapes=[
                pltpu.VMEM((4, 512, 128), F32),
                pltpu.VMEM((4, HD, 512), BF),
                pltpu.VMEM((HD, 1), F32),
            ],
        ),
        compiler_params=params(),
        cost_estimate=LIGHT,
        name="back_head",
    )(sc, *qt[1:], *q[1:], *kv, *kvt, *[dts] * 3, *lses, dq0, dkv, bias0, *xs)


def row_mean(v):
    return jnp.mean(v, axis=1, keepdims=True)


def norm(rows):
    center = rows - row_mean(rows)
    spread = lax.rsqrt(row_mean(center * center) + EPS)
    return center * spread, spread


def norm_back(grad, normed, spread, gain):
    scaled = grad * gain
    return spread * (scaled - row_mean(scaled) - normed * row_mean(scaled * normed))


def middle_kernel(few, sc, *refs):
    m0, m1, m2, m3, x_ref, cot_ref, vec_ref, ib_ref, weights = refs[:9]
    outer = refs[9:13]
    out_ref, g1_ref, d_ref, dw_ref = refs[13:17]
    (wo_ref, n1_ref, s1_ref, hid_ref, hidb_ref, hidt_ref, acc_ref, gp_ref, act_ref, gsb_ref, gst_ref,
     dvec_ref) = refs[17:]
    step = pl.program_id(0)
    vec = lambda i: vec_ref[pl.ds(i, 1), :]
    mixed = (m0, m1, m2, m3)
    inner = lambda: weights[:, 0, :, :768].reshape(768, 768)
    outer_full = lambda: weights[:, 0, :, 768:].reshape(768, 768)
    pad = jnp.zeros((64, 512), BF)
    own_rows = 768 * few // HD

    @pl.when(step == 0)
    def _():
        for k in range(4):
            o = outer[k][:, 0].reshape(768, 768)
            wo_ref[:, k * 256 : k * 256 + 256] = jnp.concatenate(
                [o[:, h * 256 + HD : h * 256 + 2 * HD] for h in range(3)] + [jnp.zeros((768, HD), BF)], axis=1
            )
        rows = x_ref[...].astype(F32) + vec(0)
        for k in range(4):
            rows = rows + dot(mixed[k][...], wo_ref[:, k * 256 : k * 256 + 192], 0, 1)
        n1, s1 = norm(rows)
        hidden = n1 * vec(1) + vec(2)
        n1_ref[...] = n1
        s1_ref[...] = s1
        hid_ref[...] = hidden
        low = hidden.astype(BF)
        hidb_ref[...] = low
        hidt_ref[...] = low.T
        acc_ref[...] = hidden + vec(3)

    @pl.when(step < 4)
    def _():
        u = dot(hidb_ref[...], inner(), 1, 0) + ib_ref[pl.ds(step, 1), :]
        cdf = 0.5 + 0.5 * lax.erf(u * math.sqrt(0.5))
        act = (u * cdf).astype(BF)
        gp_ref[step] = cdf + u * jnp.exp(-0.5 * u * u) * (1.0 / math.sqrt(2.0 * math.pi))
        act_ref[step] = act
        acc_ref[...] += dot(act, outer_full(), 1, 1)

    @pl.when(step == 3)
    def _():
        valid = (lax.broadcasted_iota(jnp.int32, (512, 1), 0) < sc[0]).astype(F32)
        n2, s2 = norm(acc_ref[...])
        out_ref[...] = (valid * (n2 * vec(4) + vec(5))).astype(BF)
        g2 = cot_ref[...].astype(F32) * valid
        gs = norm_back(g2, n2, s2, vec(4))
        low = gs.astype(BF)
        gsb_ref[...] = low
        gst_ref[...] = low.T
        dvec_ref[pl.ds(3, 1), :] = jnp.sum(gs, axis=0, keepdims=True)
        dvec_ref[pl.ds(4, 1), :] = jnp.sum(g2 * n2, axis=0, keepdims=True)
        dvec_ref[pl.ds(5, 1), :] = jnp.sum(g2, axis=0, keepdims=True)
        acc_ref[...] = gs

    @pl.when(jnp.logical_and(step >= 4, step < 8))
    def _():
        k = 7 - step
        gi = dot(gsb_ref[...], outer_full(), 1, 0) * gp_ref[k]
        dvec_ref[pl.ds(8 + k, 1), :] = jnp.sum(gi, axis=0, keepdims=True)
        low = gi.astype(BF)
        acc_ref[...] += dot(low, inner(), 1, 1)
        at = pl.multiple_of(k * 1792, 256)
        dw_ref[:, pl.ds(at, 768)] = dot(hidt_ref[...], low, 1, 0).astype(BF)
        dw_ref[:, pl.ds(at + 768, 768)] = dot(gst_ref[...], act_ref[k], 1, 0).astype(BF)

    @pl.when(step == 8)
    def _():
        gh = acc_ref[...]
        n1 = n1_ref[...]
        g1 = norm_back(gh, n1, s1_ref[...], vec(1))
        g1_ref[...] = g1
        dvec_ref[pl.ds(0, 1), :] = jnp.sum(g1, axis=0, keepdims=True)
        dvec_ref[pl.ds(1, 1), :] = jnp.sum(gh * n1, axis=0, keepdims=True)
        dvec_ref[pl.ds(2, 1), :] = jnp.sum(gh, axis=0, keepdims=True)
        dvec_ref[pl.ds(6, 2), :] = jnp.zeros((2, 768), F32)
        dvec_ref[pl.ds(12, 4), :] = jnp.zeros((4, 768), F32)
        low = g1.astype(BF)
        lowt = low.T
        columns = dvec_ref[...].T
        lane = lax.broadcasted_iota(jnp.int32, (768, 256), 1)
        unit = lax.broadcasted_iota(jnp.int32, (768, 256), 0)
        r, l = unit_index(0), unit_index(1)
        move = (r == (l % HD) // few * own_rows + (l % HD) % few).astype(F32).astype(BF)
        shared = jnp.zeros((768, 256), F32)
        for v in range(6):
            shared = jnp.where(lane == 192 + v, columns[:, v : v + 1], shared)
        shared = shared.astype(BF).astype(F32)
        for k in range(4):
            d_ref[jnp.bitwise_xor(sc[6], k)] = dot(wo_ref[:, k * 256 : k * 256 + 192], lowt, 0, 0).astype(BF)
            full = jnp.concatenate([mixed[k][...], pad], axis=0)
            bias = jnp.where(lane - 200 == unit // HD, columns[:, 8 + k : 9 + k], 0.0).astype(BF)
            tail = dot(lowt, full, 1, 1) + shared + dot(move, bias, 1, 0)
            dw_ref[:, k * 1792 + 1536 : k * 1792 + 1792] = tail.astype(BF)


def unit_index(axis):
    return lax.broadcasted_iota(jnp.int32, (768, 768), axis)


def middle(sc, mixed, x, cot, vec, ib, weights, few):
    spec = pl.BlockSpec
    fixed = lambda shape: spec(shape, lambda i, c: (0,) * len(shape))
    once = lambda shape: spec(shape, lambda i, c: (0,) * len(shape), pipeline_mode=pl.Buffered(1))
    shape = jax.ShapeDtypeStruct
    blocks, rows = weights.shape[0], weights.shape[2]
    turn = lambda i: jnp.where(i < 4, i, jnp.where(i < 8, 7 - i, 0))
    return pl.pallas_call(
        functools.partial(middle_kernel, few),
        out_shape=[shape((512, 768), BF), shape((512, 768), F32), shape((4, 192, 512), BF)]
        + [shape((768, 7168), BF)],
        grid_spec=pltpu.PrefetchScalarGridSpec(
            num_scalar_prefetch=1,
            grid=(9,),
            in_specs=[fixed((192, 512))] * 4
            + [fixed((512, 768)), fixed((512, 768)), fixed((8, 768)), fixed((4, 768))]
            + [spec((blocks, 1, rows, 1536), lambda i, c: (0, jnp.bitwise_xor(c[6], turn(i)), 0, 0))]
            + [spec((blocks, 1, rows, 768), lambda i, c, k=k: (0, jnp.bitwise_xor(c[6], k), 0, 2)) for k in range(4)],
            out_specs=[fixed((512, 768)), fixed((512, 768)), fixed((4, 192, 512))] + [once((768, 7168))],
            scratch_shapes=[
                pltpu.VMEM((768, 1024), BF),
                pltpu.VMEM((512, 768), F32),
                pltpu.VMEM((512, 1), F32),
                pltpu.VMEM((512, 768), F32),
                pltpu.VMEM((512, 768), BF),
                pltpu.VMEM((768, 512), BF),
                pltpu.VMEM((512, 768), F32),
                pltpu.VMEM((4, 512, 768), F32),
                pltpu.VMEM((4, 512, 768), BF),
                pltpu.VMEM((512, 768), BF),
                pltpu.VMEM((768, 512), BF),
                pltpu.VMEM((16, 768), F32),
            ],
        ),
        compiler_params=params(),
        cost_estimate=LIGHT,
        name="middle",
    )(sc, *mixed, x, cot, vec, ib, *[weights] * 5)


def input_grad_kernel(heads, base_ref, w_ref, *refs):
    packets, (out, acc) = refs[:-2], refs[-2:]
    k = pl.program_id(0)

    @pl.when(k == 0)
    def _():
        acc[...] = jnp.zeros_like(acc)

    for packet, h in zip(packets, heads, strict=True):
        p = packet[0]
        p = jnp.concatenate([p[:HD], jnp.zeros((HD, 512), BF), p[HD:]], axis=0)
        acc[...] += dot(w_ref[:, 0, :, h * 256 : h * 256 + 256].reshape(768, 256), p, 1, 0)

    @pl.when(k == 3)
    def _():
        out[...] = base_ref[...] + acc[...].T


def input_grad(base, weights, packets, heads):
    blocks, _, rows, _ = weights.shape
    return pl.pallas_call(
        functools.partial(input_grad_kernel, heads),
        grid=(4,),
        out_shape=jax.ShapeDtypeStruct((512, 768), F32),
        in_specs=[whole((512, 768)), pl.BlockSpec((blocks, 1, rows, 768), lambda k: (0, k, 0, 2))]
        + [pl.BlockSpec((1, 192, 512), lambda k: (k, 0, 0))] * len(packets),
        out_specs=whole((512, 768)),
        scratch_shapes=[pltpu.VMEM((768, 512), F32)],
        compiler_params=params(),
        cost_estimate=LIGHT,
        name="input_grad",
    )(base, weights, *packets)


def body(
    tokens, cotangent, lengths, query_weight, key_weight, value_weight, query_bias, value_bias, output_weight,
    output_bias, first_gain, first_shift, inner_weight, inner_bias, outer_weight, outer_bias, second_gain, second_shift,
):
    n = lax.axis_size("dp")
    me = lax.axis_index("dp")
    rows = query_weight.shape[0]
    heads = query_weight.shape[1] // HD
    few, units = inner_bias.shape
    z = lax.axis_index("tensor")
    slots = jnp.arange(4) ^ z
    counts = jnp.clip(lengths[0] - slots * 512, 0, 512).astype(jnp.int32)
    place = jnp.stack([me & 1, me >> 1, z]).astype(jnp.int32)

    by_head = lambda w: w.reshape(rows, heads, HD)
    wide = jnp.stack(
        [by_head(query_weight), by_head(output_weight), by_head(key_weight), by_head(value_weight)], axis=2
    ).reshape(rows, heads * 256)
    small = jnp.stack([output_bias, first_gain, first_shift, outer_bias, second_gain, second_shift], axis=1)
    inner_bias = exchange(jnp.broadcast_to(inner_bias[None], (4, few, units)))
    biases = jnp.concatenate([query_bias, value_bias] + [pick(inner_bias, z ^ k) for k in range(4)], axis=1)
    used = 6 + biases.shape[1]
    biases = jnp.pad(biases, ((0, rows - few), (0, 0)))
    near = jnp.concatenate([wide, small, biases, jnp.zeros((rows, 128 - used), BF)], axis=1)

    every = jnp.concatenate([inner_weight, outer_weight, wide], axis=1)
    apart = aligned(rows)
    also = lambda a, m: jnp.concatenate([a, swap(a, "dp", m)], axis=0) if apart else a
    up, down = [tokens], [tokens]

    def hop():
        up.append(shift(up[-1], 1))
        down.append(shift(down[-1], -1))

    hop()
    near = also(near, 2)
    near, up[1], down[1], every = stage(near, up[1], down[1], every)
    every = gather_all(every)
    hop()
    near = also(near, 4)
    near, up[2], down[2] = stage(near, up[2], down[2])
    hop()
    if apart:
        at = [me ^ m for m in (0, 2, 4, 6, 1, 3, 5, 7)]
        near, where = [near, swap(near, "dp", 1)], jnp.stack(at).astype(jnp.int32) * rows
    else:
        near, where = [gather_rows(near)], jnp.zeros((1,), jnp.int32)
    tile = assemble(near, where, 128, 6).astype(F32)
    vec = jnp.pad(tile[:, :6].T, ((0, 2), (0, 0)))
    tile = tile.reshape(n, rows, 128)[:, :few, 6:used].reshape(HD, used - 6).T
    blank = jnp.zeros((heads, 2 * HD), F32)
    bias = jnp.concatenate([tile[:heads], blank, tile[heads : 2 * heads]], axis=1)[:, None, :]
    ib = tile[2 * heads :].reshape(4, units * HD)
    xs = [by_slot(up, down, k) for k in range(3)]
    made = [project(x, (near, where), bias) for x in xs]
    made, up[3], down[3] = stage(made, up[3], down[3])
    xs.append(by_slot(up, down, 3))
    made.append(project(xs[3], (near, where), bias))
    qt, q, kv, kvt = ([m[i] for m in made] for i in range(4))

    mixed, lses = [None] * 4, [None] * 4
    for s in (3, 2, 1, 0):
        mixed[s], lses[s] = attend(counts, qt[s], kv, kvt)
        if s:
            come = mixed[s + 1] if s < 3 else ()
            mixed[s], qt[s - 1], come = stage(mixed[s], qt[s - 1], come)
            if s < 3:
                mixed[s + 1] = come
            mixed[s] = swap(mixed[s], "tensor", s)
    mixed, every = stage(mixed, every)

    sc = jnp.concatenate([counts, place])
    out, g1, d_out, dw = middle(sc, mixed, tokens, cotangent, vec, ib, every, few)

    total = lax.psum_scatter(dw, "dp", scatter_dimension=0, tiled=True)
    d = exchange(d_out)
    dq0, dkv, bias0 = back_own(sc, qt[0], q[0], kv, kvt, d_out, lses[0])
    d, dq0, dkv, bias0 = stage(d, dq0, dkv, bias0)
    head = lambda h, d: back_head(h, sc, qt, q, kv, kvt, d, lses[1:], dq0, dkv, bias0, xs, few)
    packet0, *dw0 = head(0, d)
    packet0, dw0, d = stage(packet0, dw0, d)
    packet0 = exchange(packet0)
    packet1, *dw1 = head(1, d)
    packet0, packet1, dw1, d = stage(packet0, packet1, dw1, d)
    packet1 = exchange(packet1)
    packet2, *dw2 = head(2, d)
    packet1, packet2, dw2, total = stage(packet1, packet2, dw2, total)

    packet2 = exchange(packet2)
    dws = [dw0, dw1, dw2]
    joined = lambda arrays: jnp.concatenate(arrays, axis=-1)
    if apart:
        own_keep, own_got = joined([v[0] for v in dws]), swap(joined([v[1] for v in dws]), "dp", 1)
    else:
        own_keep = own_got = joined([v[0] for v in dws])
    slots = [total[:, k * 1792 : k * 1792 + 1792] for k in range(4)]
    moved = [swap(v, "tensor", k) for k, v in enumerate(slots) if k]
    ahead = input_grad(g1, every, [packet0, packet1], (0, 1))
    packet2, ahead, own_keep, own_got = stage(packet2, ahead, own_keep, own_got)
    tokens_grad = input_grad(ahead, every, [packet2], (2,))
    if apart:
        block = lambda m: own_keep[m].astype(F32) + own_got[m].astype(F32)
        passed = swap(jnp.stack([block(1), block(3)]).astype(BF), "dp", 2)
        near_by = (block(2) + passed[1].astype(F32)).astype(BF)
        own = block(0) + passed[0].astype(F32) + swap(near_by, "dp", 4).astype(F32)
    else:
        own = sum_rows(own_keep)

    sums = (slots[0].astype(F32) + moved[0].astype(F32)) + (moved[1].astype(F32) + moved[2].astype(F32))
    ffn, rest = sums[:, :1536], sums[:, 1536:]
    side = lambda i: jnp.concatenate([own[:, h * 256 + i * HD : h * 256 + i * HD + HD] for h in range(heads)], axis=1)
    return (
        out,
        tokens_grad,
        side(0),
        side(1),
        side(2),
        jnp.stack([own[:few, h * 256 + 192] for h in range(heads)], axis=1),
        jnp.stack([own[:few, h * 256 + 193] for h in range(heads)], axis=1),
        rest[:, :192],
        rest[:, 192],
        rest[:, 193],
        rest[:, 194],
        ffn[:, :768],
        rest[:few, 200 : 200 + units],
        ffn[:, 768:],
        rest[:, 195],
        rest[:, 196],
        rest[:, 197],
    )


def solution(mesh):
    table, vector, token = P("dp", "tensor"), P("dp"), P(("dp", "tensor"), None)
    return jax.shard_map(
        body,
        mesh=mesh,
        in_specs=(
            token, token, vector, table, table, table, table, table, table,
            vector, vector, vector, table, table, table, vector, vector, vector,
        ),
        out_specs=(
            token, token, table, table, table, table, table, table,
            vector, vector, vector, table, table, table, vector, vector, vector,
        ),
        check_vma=False,
    )
```

```python
import functools
import math

import jax
import jax.numpy as jnp
from jax import lax
from jax.experimental import pallas as pl
from jax.experimental.pallas import tpu as pltpu
from jax.sharding import PartitionSpec as P

HD = 64
SLOT_LEN = 2048
EPS = 1e-05
NEG = -1e30
BF = jnp.bfloat16
F32 = jnp.float32
VMEM_LIMIT = 60 * 1024 * 1024
LIGHT = pl.CostEstimate(flops=1, transcendentals=0, bytes_accessed=1)


def dot(a, b, ca, cb):
    return lax.dot_general(a, b, (((ca,), (cb,)), ((), ())), preferred_element_type=F32)


def whole(shape):
    return pl.BlockSpec(shape, lambda *_: (0,) * len(shape))


def params():
    return pltpu.CompilerParams(vmem_limit_bytes=VMEM_LIMIT)


def swap(x, axis, mask):
    n = lax.axis_size(axis)
    return lax.ppermute(x, axis, [(i, i ^ mask) for i in range(n)])


def dp_groups():
    n, bit, groups = lax.axis_size("dp"), 2, []
    while bit < n:
        if bit * 2 < n:
            groups.append((bit, bit * 2, bit * 3))
            bit *= 4
        else:
            groups.append((bit,))
            bit *= 2
    return groups


def stage(*values):
    return lax.optimization_barrier(values)


def shift(x, by):
    n = lax.axis_size("tensor")
    return lax.ppermute(x, "tensor", [(i, i + by) for i in range(n) if 0 <= i + by < n])


def by_slot(up, down, k):
    z = lax.axis_index("tensor")
    odd, high = z % 2 == 1, z >= 2
    if k == 0:
        return up[0]
    if k == 1:
        return jnp.where(odd, up[1], down[1])
    if k == 2:
        return jnp.where(high, up[2], down[2])
    return jnp.where(odd, jnp.where(high, up[3], down[1]), jnp.where(high, up[1], down[3]))


def exchange(blocks):
    return lax.all_to_all(blocks, "tensor", 0, 0)


def aligned(rows):
    return rows % 16 == 0 and lax.axis_size("dp") == 8


def gather_all(piece):
    n, t = lax.axis_size("dp"), lax.axis_size("tensor")
    rows, cols = piece.shape
    blocks = lax.all_gather(piece, ("dp", "tensor")).reshape(n, t, rows, cols)
    if aligned(rows):
        return blocks
    return blocks.transpose(1, 0, 2, 3).reshape(1, t, n * rows, cols)


def gather_rows(piece):
    rows, cols = piece.shape
    n = lax.axis_size("dp")
    me = lax.axis_index("dp")
    pieces = [((0,), piece)]
    for group in dp_groups():
        if len(pieces) > 1:
            pieces = [(sum((m for m, _ in pieces), ()), jnp.concatenate([a for _, a in pieces], axis=0))]
        masks, array = pieces[0]
        pieces += [(tuple(m ^ g for m in masks), swap(array, "dp", g)) for g in group]
    pieces += [(tuple(m ^ 1 for m in masks), swap(array, "dp", 1)) for masks, array in pieces]
    order = [m for masks, _ in pieces for m in masks]
    place = [order.index(m) for m in range(n)]
    stacked = jnp.concatenate([a for _, a in pieces], axis=0).reshape(n, rows, cols)
    index = jnp.take(jnp.array(place, jnp.int32), me ^ jnp.arange(n))
    return jnp.take(stacked, index, axis=0).reshape(n * rows, cols)


def put(where, refs, out):
    if len(refs) == 1:
        out[...] = refs[0][...]
        return
    count = out.shape[0] // refs[0].shape[0]
    each = (where.shape[0] if hasattr(where, "shape") else len(where)) // count
    rows = refs[0].shape[0] // each
    for s, ref in enumerate(refs):
        for b in range(each):
            out[pl.ds(pl.multiple_of(where[each * s + b], rows), rows), :] = ref[b * rows : (b + 1) * rows]


def assemble_kernel(where, *refs):
    put(where, refs[:-1], refs[-1])


def assemble(pieces, where, block, at):
    rows, n = pieces[0].shape[0], len(pieces)
    return pl.pallas_call(
        assemble_kernel,
        out_shape=jax.ShapeDtypeStruct((n * rows, block), pieces[0].dtype),
        grid_spec=pltpu.PrefetchScalarGridSpec(
            num_scalar_prefetch=1,
            grid=(1,),
            in_specs=[pl.BlockSpec((rows, block), lambda i, w: (0, at))] * n,
            out_specs=pl.BlockSpec((n * rows, block), lambda i, w: (0, 0)),
        ),
        compiler_params=params(),
        cost_estimate=LIGHT,
        name="assemble",
    )(where, *pieces)


def split_rows(place, value, keep, send, lane):
    lanes = slice(lane, lane + value.shape[1])
    if send is None:
        keep[:, lanes] = value
        return
    rows = keep.shape[1]
    for j in range(4):
        at = jnp.bitwise_xor(j, place[1])
        even, odd = value[2 * j * rows : (2 * j + 1) * rows], value[(2 * j + 1) * rows : (2 * j + 2) * rows]
        keep[at, :, lanes] = jnp.where(place[0] == 0, even, odd)
        send[at, :, lanes] = jnp.where(place[0] == 0, odd, even)


def add_kernel(groups, *refs):
    outs = refs[len(refs) - len(groups) :]
    for out, terms in zip(outs, groups, strict=True):
        total = refs[terms[0]][...].astype(F32)
        for t in terms[1:]:
            total = total + refs[t][...].astype(F32)
        out[...] = total.reshape(out.shape).astype(out.dtype)


def add(terms, outs):
    lanes = outs[0][1]
    block = 1792
    specs = []
    for array, lead, start in terms:
        rows = array.shape[-2]
        if lead is None:
            specs.append(pl.BlockSpec((rows, block), lambda i, s=start // block: (0, i + s)))
        else:
            specs.append(pl.BlockSpec((1, rows, block), lambda i, m=lead, s=start // block: (m, 0, i + s)))
    rows = terms[0][0].shape[-2]
    return pl.pallas_call(
        functools.partial(add_kernel, [numbers for numbers, _, _ in outs]),
        grid=(lanes // block,),
        out_shape=[jax.ShapeDtypeStruct((rows, lanes), d) for _, _, d in outs],
        in_specs=specs,
        out_specs=[pl.BlockSpec((rows, block), lambda i: (0, i))] * len(outs),
        compiler_params=params(),
        cost_estimate=LIGHT,
        name="add",
    )(*[a for a, _, _ in terms])


def sum_rows(array):
    n = lax.axis_size("dp")
    me = lax.axis_index("dp")
    halves = array.reshape(n // 2, 2, array.shape[0] // n, array.shape[1])
    side = lambda c: lax.dynamic_index_in_dim(halves, c, 1, keepdims=False)
    total = side(me & 1).astype(F32) + swap(side(1 - (me & 1)), "dp", 1).astype(F32)
    for group in reversed(dp_groups()):
        count = len(group) + 1
        total = total.reshape(count, -1, *total.shape[1:])
        mine = (me // group[0]) % count
        sent = total.astype(BF)
        terms = [swap(pick(sent, mine ^ (g // group[0])), "dp", g).astype(F32) for g in group]
        total = pick(total, mine)
        for t in terms:
            total = total + t
    return total.reshape(total.shape[-2:])


def pick(array, index):
    return lax.dynamic_index_in_dim(array, index, 0, keepdims=False)


def split_shapes(aligned_rows, rows, cols):
    shape = jax.ShapeDtypeStruct
    return [shape((4, rows, cols), BF)] * 2 if aligned_rows else [shape((768, cols), BF)]


def spread(rows, few):
    i = lax.broadcasted_iota(jnp.int32, (768, HD), 1)
    r = lax.broadcasted_iota(jnp.int32, (768, HD), 0)
    return (r == (i // few) * rows + i % few).astype(F32).astype(BF)


def project_kernel(where, x_ref, b_ref, *refs):
    pieces, (qt_ref, q_ref, kv_ref, kvt_ref, w) = refs[:-5], refs[-5:]
    put(where, pieces, w)
    y = dot(x_ref[...], w[...], 1, 0) + b_ref[0]
    keep = lax.broadcasted_iota(jnp.int32, (512, 128), 1) < HD
    q = jnp.where(keep, y[:, :128].astype(BF).astype(F32) * 0.125, 0.0).astype(BF)
    kv = y[:, 128:].astype(BF)
    q_ref[0] = q
    qt_ref[0] = q.T
    kv_ref[0] = kv
    kvt_ref[0] = kv.T


def project(x, near, bias):
    pieces, where = near
    heads, rows = bias.shape[0], pieces[0].shape[0]
    shapes = [(heads, 128, 512), (heads, 512, 128), (heads, 512, 128), (heads, 128, 512)]
    return pl.pallas_call(
        project_kernel,
        out_shape=[jax.ShapeDtypeStruct(s, BF) for s in shapes],
        grid_spec=pltpu.PrefetchScalarGridSpec(
            num_scalar_prefetch=1,
            grid=(heads,),
            in_specs=[whole((512, 768)), pl.BlockSpec((1, 1, 256), lambda h, w: (h, 0, 0))]
            + [pl.BlockSpec((rows, 256), lambda h, w: (0, h))] * len(pieces),
            out_specs=[pl.BlockSpec((1, *s[1:]), lambda h, w: (h, 0, 0)) for s in shapes],
            scratch_shapes=[pltpu.VMEM((768, 256), BF)],
        ),
        compiler_params=params(),
        cost_estimate=LIGHT,
        name="project",
    )(where, x, bias, *pieces)


def masked(scores, count):
    return jnp.where(lax.broadcasted_iota(jnp.int32, scores.shape, 0) < count, scores, NEG)


def attend_kernel(counts, qt_ref, k0, k1, k2, k3, t0, t1, t2, t3, mt_ref, lse_ref):
    h = pl.program_id(0)
    qt = qt_ref[0]
    kvt = (t0, t1, t2, t3)
    scores = [masked(dot(k[0], qt, 1, 0), counts[j]) for j, k in enumerate((k0, k1, k2, k3))]
    peak = functools.reduce(jnp.maximum, [jnp.max(s, axis=0, keepdims=True) for s in scores])
    total = jnp.zeros((1, 512), F32)
    acc = jnp.zeros((128, 512), F32)
    for j in range(4):
        expo = jnp.exp(scores[j] - peak)
        total = total + jnp.sum(expo, axis=0, keepdims=True)
        acc = acc + dot(kvt[j][0], expo.astype(BF), 1, 0)
    mt_ref[pl.ds(pl.multiple_of(h * HD, HD), HD), :] = (acc[HD:] / total).astype(BF)
    lse_ref[0] = peak + jnp.log(total)


def attend(counts, qt, kv, kvt):
    heads = qt.shape[0]
    return pl.pallas_call(
        attend_kernel,
        out_shape=[jax.ShapeDtypeStruct((heads * HD, 512), BF), jax.ShapeDtypeStruct((heads, 1, 512), F32)],
        grid_spec=pltpu.PrefetchScalarGridSpec(
            num_scalar_prefetch=1,
            grid=(heads,),
            in_specs=[pl.BlockSpec((1, 128, 512), lambda h, c: (h, 0, 0))]
            + [pl.BlockSpec((1, 512, 128), lambda h, c: (h, 0, 0))] * 4
            + [pl.BlockSpec((1, 128, 512), lambda h, c: (h, 0, 0))] * 4,
            out_specs=[
                pl.BlockSpec((heads * HD, 512), lambda h, c: (0, 0)),
                pl.BlockSpec((1, 1, 512), lambda h, c: (h, 0, 0)),
            ],
        ),
        compiler_params=params(),
        cost_estimate=LIGHT,
        name="attend",
    )(counts, qt, *kv, *kvt)


def back_step(counts, qt, q, kv, kvt, dot_rows, lse, dkv_ref, fresh):
    dt = jnp.concatenate([jnp.zeros((HD, 512), BF), dot_rows], axis=0)
    d = dt.T
    probs, grads = [], []
    inner = jnp.zeros((1, 512), F32)
    for j in range(4):
        p = jnp.exp(masked(dot(kv[j][0], qt, 1, 0), counts[j]) - lse)
        g = dot(kv[j][0], dt, 1, 0)
        inner = inner + jnp.sum(p * g, axis=0, keepdims=True)
        probs.append(p)
        grads.append(g)
    dqt = jnp.zeros((128, 512), F32)
    for j in range(4):
        ds = (probs[j] * (grads[j] - inner)).astype(BF)
        dqt = dqt + dot(kvt[j][0], ds, 1, 0)
        dkv = dot(ds, q, 1, 0) + dot(probs[j].astype(BF), d, 1, 0)
        if fresh is None:
            dkv_ref[j] = dkv
        else:
            dkv_ref[j] = dkv_ref[j] + dkv
    return dqt[:HD] * 0.125


def back_own_kernel(counts, qt_ref, q_ref, *refs):
    kv, kvt, (dt_ref, lse_ref, dqt_ref, dkv_ref, bias_ref) = refs[:4], refs[4:8], refs[8:]
    dqt = back_step(counts, qt_ref[0], q_ref[0], kv, kvt, dt_ref[0], lse_ref[0], dkv_ref.at[0], None)
    dqt_ref[0] = dqt.astype(BF)
    bias_ref[0] = jnp.sum(dqt, axis=1, keepdims=True)


def back_own(counts, qt, q, kv, kvt, dt, lse):
    heads = qt.shape[0]
    tall, flat = pl.BlockSpec((1, 512, 128), lambda h, c: (h, 0, 0)), pl.BlockSpec((1, 128, 512), lambda h, c: (h, 0, 0))
    return pl.pallas_call(
        back_own_kernel,
        out_shape=[
            jax.ShapeDtypeStruct((heads, HD, 512), BF),
            jax.ShapeDtypeStruct((heads, 4, 512, 128), F32),
            jax.ShapeDtypeStruct((heads, HD, 1), F32),
        ],
        grid_spec=pltpu.PrefetchScalarGridSpec(
            num_scalar_prefetch=1,
            grid=(heads,),
            in_specs=[flat, tall]
            + [tall] * 4
            + [flat] * 4
            + [
                pl.BlockSpec((1, HD, 512), lambda h, c: (c[6], h, 0)),
                pl.BlockSpec((1, 1, 512), lambda h, c: (h, 0, 0)),
            ],
            out_specs=[
                pl.BlockSpec((1, HD, 512), lambda h, c: (h, 0, 0)),
                pl.BlockSpec((1, 4, 512, 128), lambda h, c: (h, 0, 0, 0)),
                pl.BlockSpec((1, HD, 1), lambda h, c: (h, 0, 0)),
            ],
        ),
        compiler_params=params(),
        cost_estimate=LIGHT,
        name="back_own",
    )(counts, qt, q, *kv, *kvt, dt, lse)


def back_head_kernel(few, apart, sc, *refs):
    qts, qs, kv, kvt = refs[:3], refs[3:6], refs[6:10], refs[10:14]
    ds, ls, (dq0_ref, dkv_ref, b_ref), xs = refs[14:17], refs[17:20], refs[20:23], refs[23:27]
    packet, outs, (acc, dqs, qb) = refs[27], refs[28:-3], refs[-3:]
    s = pl.program_id(0)

    @pl.when(s == 0)
    def _():
        acc[...] = dkv_ref[0]
        dqs[0] = dq0_ref[0]
        qb[...] = b_ref[0]

    choose = lambda a: jnp.where(s == 0, a[0], jnp.where(s == 1, a[1], a[2]))
    rows = choose([d[0] for d in ds])
    lse = choose([v[0] for v in ls])
    qt, q = choose([v[0] for v in qts]), choose([v[0] for v in qs])
    dqt = back_step(sc, qt, q, kv, kvt, rows, lse, acc, True)
    dqs[s + 1] = dqt.astype(BF)
    qb[...] += jnp.sum(dqt, axis=1, keepdims=True)

    @pl.when(s == 2)
    def _():
        dwt = jnp.zeros((256, 768), F32)
        vsum = jnp.zeros((1, 128), F32)
        for j in range(4):
            part = acc[j]
            vsum = vsum + jnp.sum(part, axis=0, keepdims=True)
            both = jnp.concatenate([dqs[j], part.astype(BF).T], axis=0)
            packet[jnp.bitwise_xor(sc[6], j)] = both
            both = jnp.concatenate([both, jnp.zeros((HD, 512), BF)], axis=0)
            dwt = dwt + dot(both, xs[j][...], 1, 0)
        lane = lax.broadcasted_iota(jnp.int32, (HD, 256), 1)
        vcol = jnp.broadcast_to(vsum, (128, 128)).T[HD:, :1]
        sums = jnp.where(lane == 192, qb[...], jnp.where(lane == 193, vcol, 0.0)).astype(BF)
        rows = 768 * few // HD
        dw = dwt.T + dot(spread(rows, few), sums, 1, 0)
        split_rows((sc[4], sc[5]), dw.astype(BF), outs[0], outs[1] if apart else None, 0)


def back_head(h, sc, qt, q, kv, kvt, dts, lses, dq0, dkv, bias0, xs, few):
    spec = pl.BlockSpec
    rows = 768 * few // HD
    apart = aligned(rows)
    tall, flat = spec((1, 512, 128), lambda s, c: (h, 0, 0)), spec((1, 128, 512), lambda s, c: (h, 0, 0))
    splits = split_shapes(apart, rows, 256)
    return pl.pallas_call(
        functools.partial(back_head_kernel, few, apart),
        out_shape=[jax.ShapeDtypeStruct((4, 3 * HD, 512), BF)] + splits,
        grid_spec=pltpu.PrefetchScalarGridSpec(
            num_scalar_prefetch=1,
            grid=(3,),
            in_specs=[flat] * 3
            + [tall] * 3
            + [tall] * 4
            + [flat] * 4
            + [spec((1, HD, 512), lambda s, c, j=j: (jnp.bitwise_xor(c[6], j), h, 0)) for j in (1, 2, 3)]
            + [spec((1, 1, 512), lambda s, c: (h, 0, 0))] * 3
            + [
                spec((1, HD, 512), lambda s, c: (h, 0, 0)),
                spec((1, 4, 512, 128), lambda s, c: (h, 0, 0, 0)),
                spec((1, HD, 1), lambda s, c: (h, 0, 0)),
            ]
            + [spec((512, 768), lambda s, c: (0, 0))] * 4,
            out_specs=[spec((4, 3 * HD, 512), lambda s, c: (0, 0, 0))]
            + [spec(v.shape, lambda s, c, d=len(v.shape): (0,) * d) for v in splits],
            scratch_shapes=[
                pltpu.VMEM((4, 512, 128), F32),
                pltpu.VMEM((4, HD, 512), BF),
                pltpu.VMEM((HD, 1), F32),
            ],
        ),
        compiler_params=params(),
        cost_estimate=LIGHT,
        name="back_head",
    )(sc, *qt[1:], *q[1:], *kv, *kvt, *[dts] * 3, *lses, dq0, dkv, bias0, *xs)


def row_mean(v):
    return jnp.mean(v, axis=1, keepdims=True)


def norm(rows):
    center = rows - row_mean(rows)
    spread = lax.rsqrt(row_mean(center * center) + EPS)
    return center * spread, spread


def norm_back(grad, normed, spread, gain):
    scaled = grad * gain
    return spread * (scaled - row_mean(scaled) - normed * row_mean(scaled * normed))


def middle_kernel(few, sc, *refs):
    m0, m1, m2, m3, x_ref, cot_ref, vec_ref, weights = refs[:8]
    outer = refs[8:12]
    out_ref, g1_ref, d_ref = refs[12:15]
    dw_ref = refs[15]
    (wo_ref, n1_ref, s1_ref, hid_ref, hidb_ref, hidt_ref, acc_ref, gp_ref, act_ref, gsb_ref, gst_ref,
     dvec_ref, ib_ref, move_ref) = refs[16:]
    step = pl.program_id(0)
    vec = lambda i: vec_ref[pl.ds(i, 1), :]
    mixed = (m0, m1, m2, m3)
    inner = lambda: weights[:, 0, :, :768].reshape(768, 768)
    outer_full = lambda: weights[:, 0, :, 768:].reshape(768, 768)
    pad = jnp.zeros((64, 512), BF)
    own_rows = 768 * few // HD

    @pl.when(step == 0)
    def _():
        for k in range(4):
            wo_ref[:, k * 256 : k * 256 + 256] = outer[k][:, 0].reshape(768, 256)
        r, l = unit_index(0), unit_index(1)
        move_ref[...] = (r == (l % HD) // few * own_rows + (l % HD) % few).astype(F32).astype(BF)
        unit = lax.broadcasted_iota(jnp.int32, (128, 768), 0)
        lane = lax.broadcasted_iota(jnp.int32, (128, 768), 1)
        for k in range(4):
            spread = dot(wo_ref[:, k * 256 + 128 : k * 256 + 256], move_ref[...], 0, 0)
            ib_ref[k : k + 1] = jnp.sum(jnp.where(unit - 64 == lane // HD, spread, 0.0), axis=0, keepdims=True)
        rows = x_ref[...].astype(F32) + vec(0)
        for k in range(4):
            rows = rows + dot(mixed[k][...], wo_ref[:, k * 256 : k * 256 + 192], 0, 1)
        n1, s1 = norm(rows)
        hidden = n1 * vec(1) + vec(2)
        n1_ref[...] = n1
        s1_ref[...] = s1
        hid_ref[...] = hidden
        low = hidden.astype(BF)
        hidb_ref[...] = low
        hidt_ref[...] = low.T
        acc_ref[...] = hidden + vec(3)

    @pl.when(step < 4)
    def _():
        u = dot(hidb_ref[...], inner(), 1, 0) + ib_ref[pl.ds(step, 1), :]
        cdf = 0.5 + 0.5 * lax.erf(u * math.sqrt(0.5))
        act = (u * cdf).astype(BF)
        gp_ref[step] = cdf + u * jnp.exp(-0.5 * u * u) * (1.0 / math.sqrt(2.0 * math.pi))
        act_ref[step] = act
        acc_ref[...] += dot(act, outer_full(), 1, 1)

    @pl.when(step == 3)
    def _():
        valid = (lax.broadcasted_iota(jnp.int32, (512, 1), 0) < sc[0]).astype(F32)
        n2, s2 = norm(acc_ref[...])
        out_ref[...] = (valid * (n2 * vec(4) + vec(5))).astype(BF)
        g2 = cot_ref[...].astype(F32) * valid
        gs = norm_back(g2, n2, s2, vec(4))
        low = gs.astype(BF)
        gsb_ref[...] = low
        gst_ref[...] = low.T
        dvec_ref[pl.ds(3, 1), :] = jnp.sum(gs, axis=0, keepdims=True)
        dvec_ref[pl.ds(4, 1), :] = jnp.sum(g2 * n2, axis=0, keepdims=True)
        dvec_ref[pl.ds(5, 1), :] = jnp.sum(g2, axis=0, keepdims=True)
        acc_ref[...] = gs

    @pl.when(jnp.logical_and(step >= 4, step < 8))
    def _():
        k = 7 - step
        gi = dot(gsb_ref[...], outer_full(), 1, 0) * gp_ref[k]
        dvec_ref[pl.ds(8 + k, 1), :] = jnp.sum(gi, axis=0, keepdims=True)
        low = gi.astype(BF)
        acc_ref[...] += dot(low, inner(), 1, 1)
        at = pl.multiple_of(k * 1792, 256)
        dw_ref[:, pl.ds(at, 768)] = dot(hidt_ref[...], low, 1, 0).astype(BF)
        dw_ref[:, pl.ds(at + 768, 768)] = dot(gst_ref[...], act_ref[k], 1, 0).astype(BF)

    @pl.when(step == 8)
    def _():
        gh = acc_ref[...]
        n1 = n1_ref[...]
        g1 = norm_back(gh, n1, s1_ref[...], vec(1))
        g1_ref[...] = g1
        dvec_ref[pl.ds(0, 1), :] = jnp.sum(g1, axis=0, keepdims=True)
        dvec_ref[pl.ds(1, 1), :] = jnp.sum(gh * n1, axis=0, keepdims=True)
        dvec_ref[pl.ds(2, 1), :] = jnp.sum(gh, axis=0, keepdims=True)
        dvec_ref[pl.ds(6, 2), :] = jnp.zeros((2, 768), F32)
        dvec_ref[pl.ds(12, 4), :] = jnp.zeros((4, 768), F32)
        low = g1.astype(BF)
        lowt = low.T
        columns = dvec_ref[...].T
        lane = lax.broadcasted_iota(jnp.int32, (768, 256), 1)
        unit = lax.broadcasted_iota(jnp.int32, (768, 256), 0)
        shared = jnp.zeros((768, 256), F32)
        for v in range(6):
            shared = jnp.where(lane == 192 + v, columns[:, v : v + 1], shared)
        shared = shared.astype(BF).astype(F32)
        for k in range(4):
            d_ref[jnp.bitwise_xor(sc[6], k)] = dot(wo_ref[:, k * 256 : k * 256 + 192], lowt, 0, 0).astype(BF)
            full = jnp.concatenate([mixed[k][...], pad], axis=0)
            bias = jnp.where(lane - 200 == unit // HD, columns[:, 8 + k : 9 + k], 0.0).astype(BF)
            tail = dot(lowt, full, 1, 1) + shared + dot(move_ref[...], bias, 1, 0)
            dw_ref[:, k * 1792 + 1536 : k * 1792 + 1792] = tail.astype(BF)


def unit_index(axis):
    return lax.broadcasted_iota(jnp.int32, (768, 768), axis)


def middle(sc, mixed, x, cot, vec, weights, few):
    spec = pl.BlockSpec
    fixed = lambda shape: spec(shape, lambda i, c: (0,) * len(shape))
    once = lambda shape: spec(shape, lambda i, c: (0,) * len(shape), pipeline_mode=pl.Buffered(1))
    shape = jax.ShapeDtypeStruct
    blocks, rows = weights.shape[0], weights.shape[2]
    turn = lambda i: jnp.where(i < 4, i, jnp.where(i < 8, 7 - i, 0))
    return pl.pallas_call(
        functools.partial(middle_kernel, few),
        out_shape=[shape((512, 768), BF), shape((512, 768), F32), shape((4, 192, 512), BF)]
        + [shape((768, 7168), BF)],
        grid_spec=pltpu.PrefetchScalarGridSpec(
            num_scalar_prefetch=1,
            grid=(9,),
            in_specs=[fixed((192, 512))] * 4
            + [fixed((512, 768)), fixed((512, 768)), fixed((8, 768))]
            + [spec((blocks, 1, rows, 1536), lambda i, c: (0, jnp.bitwise_xor(c[6], turn(i)), 0, 0))]
            + [spec((blocks, 1, rows, 256), lambda i, c, k=k: (0, jnp.bitwise_xor(c[6], k), 0, 6)) for k in range(4)],
            out_specs=[fixed((512, 768)), fixed((512, 768)), fixed((4, 192, 512))] + [once((768, 7168))],
            scratch_shapes=[
                pltpu.VMEM((768, 1024), BF),
                pltpu.VMEM((512, 768), F32),
                pltpu.VMEM((512, 1), F32),
                pltpu.VMEM((512, 768), F32),
                pltpu.VMEM((512, 768), BF),
                pltpu.VMEM((768, 512), BF),
                pltpu.VMEM((512, 768), F32),
                pltpu.VMEM((4, 512, 768), F32),
                pltpu.VMEM((4, 512, 768), BF),
                pltpu.VMEM((512, 768), BF),
                pltpu.VMEM((768, 512), BF),
                pltpu.VMEM((16, 768), F32),
                pltpu.VMEM((8, 768), F32),
                pltpu.VMEM((768, 768), BF),
            ],
        ),
        compiler_params=params(),
        cost_estimate=LIGHT,
        name="middle",
    )(sc, *mixed, x, cot, vec, *[weights] * 5)


def input_grad_kernel(heads, base_ref, w_ref, *refs):
    packets, (out, acc) = refs[:-2], refs[-2:]
    k = pl.program_id(0)

    @pl.when(k == 0)
    def _():
        acc[...] = jnp.zeros_like(acc)

    for packet, h in zip(packets, heads, strict=True):
        p = packet[0]
        p = jnp.concatenate([p[:HD], jnp.zeros((HD, 512), BF), p[HD:]], axis=0)
        acc[...] += dot(w_ref[:, 0, :, h * 256 : h * 256 + 256].reshape(768, 256), p, 1, 0)

    @pl.when(k == 3)
    def _():
        out[...] = base_ref[...] + acc[...].T


def input_grad(base, weights, packets, heads):
    blocks, _, rows, _ = weights.shape
    return pl.pallas_call(
        functools.partial(input_grad_kernel, heads),
        grid=(4,),
        out_shape=jax.ShapeDtypeStruct((512, 768), F32),
        in_specs=[whole((512, 768)), pl.BlockSpec((blocks, 1, rows, 768), lambda k: (0, k, 0, 0))]
        + [pl.BlockSpec((1, 192, 512), lambda k: (k, 0, 0))] * len(packets),
        out_specs=whole((512, 768)),
        scratch_shapes=[pltpu.VMEM((768, 512), F32)],
        compiler_params=params(),
        cost_estimate=LIGHT,
        name="input_grad",
    )(base, weights, *packets)


def body(
    tokens, cotangent, lengths, query_weight, key_weight, value_weight, query_bias, value_bias, output_weight,
    output_bias, first_gain, first_shift, inner_weight, inner_bias, outer_weight, outer_bias, second_gain, second_shift,
):
    n = lax.axis_size("dp")
    me = lax.axis_index("dp")
    rows = query_weight.shape[0]
    heads = query_weight.shape[1] // HD
    few, units = inner_bias.shape
    z = lax.axis_index("tensor")
    slots = jnp.arange(4) ^ z
    counts = jnp.clip(lengths[0] - slots * 512, 0, 512).astype(jnp.int32)
    place = jnp.stack([me & 1, me >> 1, z]).astype(jnp.int32)

    by_head = lambda w: w.reshape(rows, heads, HD)
    wide = jnp.stack(
        [by_head(query_weight), by_head(output_weight), by_head(key_weight), by_head(value_weight)], axis=2
    ).reshape(rows, heads * 256)
    small = jnp.stack([output_bias, first_gain, first_shift, outer_bias, second_gain, second_shift], axis=1)
    biases = jnp.pad(jnp.concatenate([query_bias, value_bias], axis=1), ((0, rows - few), (0, 0)))
    used = 6 + 2 * heads
    near = jnp.concatenate([wide, small, biases, jnp.zeros((rows, 128 - used), BF)], axis=1)

    extra = jnp.pad(inner_bias, ((0, rows - few), (0, 64 - units)))
    front = jnp.concatenate([inner_weight, outer_weight, output_weight, extra], axis=1)
    apart = aligned(rows)
    also = lambda a, m: jnp.concatenate([a, swap(a, "dp", m)], axis=0) if apart else a
    up, down = [tokens], [tokens]

    def hop():
        up.append(shift(up[-1], 1))
        down.append(shift(down[-1], -1))

    hop()
    near = also(near, 2)
    near, up[1], down[1], front = stage(near, up[1], down[1], front)
    front = gather_all(front)
    hop()
    near = also(near, 4)
    near, up[2], down[2], later = stage(near, up[2], down[2], wide)
    full = gather_all(later)
    hop()
    if apart:
        at = [me ^ m for m in (0, 2, 4, 6, 1, 3, 5, 7)]
        near, where = [near, swap(near, "dp", 1)], jnp.stack(at).astype(jnp.int32) * rows
    else:
        near, where = [gather_rows(near)], jnp.zeros((1,), jnp.int32)
    tile = assemble(near, where, 128, 6).astype(F32)
    vec = jnp.pad(tile[:, :6].T, ((0, 2), (0, 0)))
    tile = tile.reshape(n, rows, 128)[:, :few, 6:used].reshape(HD, used - 6).T
    blank = jnp.zeros((heads, 2 * HD), F32)
    bias = jnp.concatenate([tile[:heads], blank, tile[heads:]], axis=1)[:, None, :]
    xs = [by_slot(up, down, k) for k in range(3)]
    made = [project(x, (near, where), bias) for x in xs]
    made, up[3], down[3] = stage(made, up[3], down[3])
    xs.append(by_slot(up, down, 3))
    made.append(project(xs[3], (near, where), bias))
    qt, q, kv, kvt = ([m[i] for m in made] for i in range(4))

    mixed, lses = [None] * 4, [None] * 4
    for s in (3, 2, 1, 0):
        mixed[s], lses[s] = attend(counts, qt[s], kv, kvt)
        if s:
            come = mixed[s + 1] if s < 3 else ()
            mixed[s], qt[s - 1], come = stage(mixed[s], qt[s - 1], come)
            if s < 3:
                mixed[s + 1] = come
            mixed[s] = swap(mixed[s], "tensor", s)
    mixed, front = stage(mixed, front)

    sc = jnp.concatenate([counts, place])
    out, g1, d_out, dw = middle(sc, mixed, tokens, cotangent, vec, front, few)

    d = exchange(d_out)
    dq0, dkv, bias0 = back_own(sc, qt[0], q[0], kv, kvt, d_out, lses[0])
    dw, full, d, dq0, dkv, bias0 = stage(dw, full, d, dq0, dkv, bias0)
    total = lax.psum_scatter(dw, "dp", scatter_dimension=0, tiled=True)
    head = lambda h, d: back_head(h, sc, qt, q, kv, kvt, d, lses[1:], dq0, dkv, bias0, xs, few)
    packet0, *dw0 = head(0, d)
    packet0, dw0, d = stage(packet0, dw0, d)
    packet0 = exchange(packet0)
    packet1, *dw1 = head(1, d)
    packet0, packet1, dw1, d = stage(packet0, packet1, dw1, d)
    packet1 = exchange(packet1)
    packet2, *dw2 = head(2, d)
    packet1, packet2, dw2 = stage(packet1, packet2, dw2)

    packet2 = exchange(packet2)
    dws = [dw0, dw1, dw2]
    joined = lambda arrays: jnp.concatenate(arrays, axis=-1)
    if apart:
        keep, got = joined([v[0] for v in dws]), swap(joined([v[1] for v in dws]), "dp", 1)
        block = lambda m: keep[m].astype(F32) + got[m].astype(F32)
        passed = swap(jnp.stack([block(1), block(3)]).astype(BF), "dp", 2)
        near_by = (block(2) + passed[1].astype(F32)).astype(BF)
        own = block(0) + passed[0].astype(F32)
    else:
        own, near_by = joined([v[0] for v in dws]), ()
    ahead = input_grad(g1, full, [packet0, packet1], (0, 1))
    ahead, own, near_by, total, packet2 = stage(ahead, own, near_by, total, packet2)
    slots = [total[:, k * 1792 : k * 1792 + 1792] for k in range(4)]
    moved = [swap(v, "tensor", k) for k, v in enumerate(slots) if k]
    own = own + swap(near_by, "dp", 4).astype(F32) if apart else sum_rows(own)
    tokens_grad = input_grad(ahead, full, [packet2], (2,))
    side = lambda i: jnp.concatenate([own[:, h * 256 + i * HD : h * 256 + i * HD + HD] for h in range(heads)], axis=1)
    sides = [side(i) for i in range(3)]
    qb = jnp.stack([own[:few, h * 256 + 192] for h in range(heads)], axis=1)
    vb = jnp.stack([own[:few, h * 256 + 193] for h in range(heads)], axis=1)
    tokens_grad, sides, qb, vb, moved = stage(tokens_grad, sides, qb, vb, moved)

    sums = (slots[0].astype(F32) + moved[0].astype(F32)) + (moved[1].astype(F32) + moved[2].astype(F32))
    ffn, rest = sums[:, :1536], sums[:, 1536:]
    return (
        out,
        tokens_grad,
        *sides,
        qb,
        vb,
        rest[:, :192],
        rest[:, 192],
        rest[:, 193],
        rest[:, 194],
        ffn[:, :768],
        rest[:few, 200 : 200 + units],
        ffn[:, 768:],
        rest[:, 195],
        rest[:, 196],
        rest[:, 197],
    )


def solution(mesh):
    table, vector, token = P("dp", "tensor"), P("dp"), P(("dp", "tensor"), None)
    return jax.shard_map(
        body,
        mesh=mesh,
        in_specs=(
            token, token, vector, table, table, table, table, table, table,
            vector, vector, vector, table, table, table, vector, vector, vector,
        ),
        out_specs=(
            token, token, table, table, table, table, table, table,
            vector, vector, vector, table, table, table, vector, vector, vector,
        ),
        check_vma=False,
    )
```

```python
import functools
import math

import jax
import jax.numpy as jnp
from jax import lax
from jax.experimental import pallas as pl
from jax.experimental.pallas import tpu as pltpu
from jax.sharding import PartitionSpec as P

HD = 64
SLOT_LEN = 2048
EPS = 1e-05
NEG = -1e30
BF = jnp.bfloat16
F32 = jnp.float32
VMEM_LIMIT = 60 * 1024 * 1024
LIGHT = pl.CostEstimate(flops=1, transcendentals=0, bytes_accessed=1)


def dot(a, b, ca, cb):
    return lax.dot_general(a, b, (((ca,), (cb,)), ((), ())), preferred_element_type=F32)


def whole(shape):
    return pl.BlockSpec(shape, lambda *_: (0,) * len(shape))


def params():
    return pltpu.CompilerParams(vmem_limit_bytes=VMEM_LIMIT)


def swap(x, axis, mask):
    n = lax.axis_size(axis)
    return lax.ppermute(x, axis, [(i, i ^ mask) for i in range(n)])


def dp_groups():
    n, bit, groups = lax.axis_size("dp"), 2, []
    while bit < n:
        if bit * 2 < n:
            groups.append((bit, bit * 2, bit * 3))
            bit *= 4
        else:
            groups.append((bit,))
            bit *= 2
    return groups


def stage(*values):
    return lax.optimization_barrier(values)


def shift(x, by):
    n = lax.axis_size("tensor")
    return lax.ppermute(x, "tensor", [(i, i + by) for i in range(n) if 0 <= i + by < n])


def by_slot(up, down, k):
    z = lax.axis_index("tensor")
    odd, high = z % 2 == 1, z >= 2
    if k == 0:
        return up[0]
    if k == 1:
        return jnp.where(odd, up[1], down[1])
    if k == 2:
        return jnp.where(high, up[2], down[2])
    return jnp.where(odd, jnp.where(high, up[3], down[1]), jnp.where(high, up[1], down[3]))


def exchange(blocks):
    return lax.all_to_all(blocks, "tensor", 0, 0)


def aligned(rows):
    return rows % 16 == 0 and lax.axis_size("dp") == 8


def gather_all(piece):
    n, t = lax.axis_size("dp"), lax.axis_size("tensor")
    rows, cols = piece.shape
    blocks = lax.all_gather(piece, ("dp", "tensor")).reshape(n, t, rows, cols)
    if aligned(rows):
        return blocks
    return blocks.transpose(1, 0, 2, 3).reshape(1, t, n * rows, cols)


def gather_rows(piece):
    rows, cols = piece.shape
    n = lax.axis_size("dp")
    me = lax.axis_index("dp")
    pieces = [((0,), piece)]
    for group in dp_groups():
        if len(pieces) > 1:
            pieces = [(sum((m for m, _ in pieces), ()), jnp.concatenate([a for _, a in pieces], axis=0))]
        masks, array = pieces[0]
        pieces += [(tuple(m ^ g for m in masks), swap(array, "dp", g)) for g in group]
    pieces += [(tuple(m ^ 1 for m in masks), swap(array, "dp", 1)) for masks, array in pieces]
    order = [m for masks, _ in pieces for m in masks]
    place = [order.index(m) for m in range(n)]
    stacked = jnp.concatenate([a for _, a in pieces], axis=0).reshape(n, rows, cols)
    index = jnp.take(jnp.array(place, jnp.int32), me ^ jnp.arange(n))
    return jnp.take(stacked, index, axis=0).reshape(n * rows, cols)


def put(where, refs, out):
    if len(refs) == 1:
        out[...] = refs[0][...]
        return
    count = out.shape[0] // refs[0].shape[0]
    each = (where.shape[0] if hasattr(where, "shape") else len(where)) // count
    rows = refs[0].shape[0] // each
    for s, ref in enumerate(refs):
        for b in range(each):
            out[pl.ds(pl.multiple_of(where[each * s + b], rows), rows), :] = ref[b * rows : (b + 1) * rows]


def assemble_kernel(where, *refs):
    put(where, refs[:-1], refs[-1])


def assemble(pieces, where, block, at):
    rows, n = pieces[0].shape[0], len(pieces)
    return pl.pallas_call(
        assemble_kernel,
        out_shape=jax.ShapeDtypeStruct((n * rows, block), pieces[0].dtype),
        grid_spec=pltpu.PrefetchScalarGridSpec(
            num_scalar_prefetch=1,
            grid=(1,),
            in_specs=[pl.BlockSpec((rows, block), lambda i, w: (0, at))] * n,
            out_specs=pl.BlockSpec((n * rows, block), lambda i, w: (0, 0)),
        ),
        compiler_params=params(),
        cost_estimate=LIGHT,
        name="assemble",
    )(where, *pieces)


def split_rows(place, value, keep, send, lane):
    lanes = slice(lane, lane + value.shape[1])
    if send is None:
        keep[:, lanes] = value
        return
    rows = keep.shape[1]
    for j in range(4):
        at = jnp.bitwise_xor(j, place[1])
        even, odd = value[2 * j * rows : (2 * j + 1) * rows], value[(2 * j + 1) * rows : (2 * j + 2) * rows]
        keep[at, :, lanes] = jnp.where(place[0] == 0, even, odd)
        send[at, :, lanes] = jnp.where(place[0] == 0, odd, even)


def add_kernel(groups, *refs):
    outs = refs[len(refs) - len(groups) :]
    for out, terms in zip(outs, groups, strict=True):
        total = refs[terms[0]][...].astype(F32)
        for t in terms[1:]:
            total = total + refs[t][...].astype(F32)
        out[...] = total.reshape(out.shape).astype(out.dtype)


def add(terms, outs):
    lanes = outs[0][1]
    block = 1792
    specs = []
    for array, lead, start in terms:
        rows = array.shape[-2]
        if lead is None:
            specs.append(pl.BlockSpec((rows, block), lambda i, s=start // block: (0, i + s)))
        else:
            specs.append(pl.BlockSpec((1, rows, block), lambda i, m=lead, s=start // block: (m, 0, i + s)))
    rows = terms[0][0].shape[-2]
    return pl.pallas_call(
        functools.partial(add_kernel, [numbers for numbers, _, _ in outs]),
        grid=(lanes // block,),
        out_shape=[jax.ShapeDtypeStruct((rows, lanes), d) for _, _, d in outs],
        in_specs=specs,
        out_specs=[pl.BlockSpec((rows, block), lambda i: (0, i))] * len(outs),
        compiler_params=params(),
        cost_estimate=LIGHT,
        name="add",
    )(*[a for a, _, _ in terms])


def sum_rows(array):
    n = lax.axis_size("dp")
    me = lax.axis_index("dp")
    halves = array.reshape(n // 2, 2, array.shape[0] // n, array.shape[1])
    side = lambda c: lax.dynamic_index_in_dim(halves, c, 1, keepdims=False)
    total = side(me & 1).astype(F32) + swap(side(1 - (me & 1)), "dp", 1).astype(F32)
    for group in reversed(dp_groups()):
        count = len(group) + 1
        total = total.reshape(count, -1, *total.shape[1:])
        mine = (me // group[0]) % count
        sent = total.astype(BF)
        terms = [swap(pick(sent, mine ^ (g // group[0])), "dp", g).astype(F32) for g in group]
        total = pick(total, mine)
        for t in terms:
            total = total + t
    return total.reshape(total.shape[-2:])


def pick(array, index):
    return lax.dynamic_index_in_dim(array, index, 0, keepdims=False)


def split_shapes(aligned_rows, rows, cols):
    shape = jax.ShapeDtypeStruct
    return [shape((4, rows, cols), BF)] * 2 if aligned_rows else [shape((768, cols), BF)]


def spread(rows, few):
    i = lax.broadcasted_iota(jnp.int32, (768, HD), 1)
    r = lax.broadcasted_iota(jnp.int32, (768, HD), 0)
    return (r == (i // few) * rows + i % few).astype(F32).astype(BF)


def project_kernel(where, x_ref, b_ref, *refs):
    pieces, (qt_ref, q_ref, kv_ref, kvt_ref, w) = refs[:-5], refs[-5:]
    put(where, pieces, w)
    y = dot(x_ref[...], w[...], 1, 0) + b_ref[0]
    keep = lax.broadcasted_iota(jnp.int32, (512, 128), 1) < HD
    q = jnp.where(keep, y[:, :128].astype(BF).astype(F32) * 0.125, 0.0).astype(BF)
    kv = y[:, 128:].astype(BF)
    q_ref[0] = q
    qt_ref[0] = q.T
    kv_ref[0] = kv
    kvt_ref[0] = kv.T


def project(x, near, bias):
    pieces, where = near
    heads, rows = bias.shape[0], pieces[0].shape[0]
    shapes = [(heads, 128, 512), (heads, 512, 128), (heads, 512, 128), (heads, 128, 512)]
    return pl.pallas_call(
        project_kernel,
        out_shape=[jax.ShapeDtypeStruct(s, BF) for s in shapes],
        grid_spec=pltpu.PrefetchScalarGridSpec(
            num_scalar_prefetch=1,
            grid=(heads,),
            in_specs=[whole((512, 768)), pl.BlockSpec((1, 1, 256), lambda h, w: (h, 0, 0))]
            + [pl.BlockSpec((rows, 256), lambda h, w: (0, h))] * len(pieces),
            out_specs=[pl.BlockSpec((1, *s[1:]), lambda h, w: (h, 0, 0)) for s in shapes],
            scratch_shapes=[pltpu.VMEM((768, 256), BF)],
        ),
        compiler_params=params(),
        cost_estimate=LIGHT,
        name="project",
    )(where, x, bias, *pieces)


def masked(scores, count):
    return jnp.where(lax.broadcasted_iota(jnp.int32, scores.shape, 0) < count, scores, NEG)


def attend_kernel(counts, qt_ref, k0, k1, k2, k3, t0, t1, t2, t3, mt_ref, lse_ref):
    h = pl.program_id(0)
    qt = qt_ref[0]
    kvt = (t0, t1, t2, t3)
    scores = [masked(dot(k[0], qt, 1, 0), counts[j]) for j, k in enumerate((k0, k1, k2, k3))]
    peak = functools.reduce(jnp.maximum, [jnp.max(s, axis=0, keepdims=True) for s in scores])
    total = jnp.zeros((1, 512), F32)
    acc = jnp.zeros((128, 512), F32)
    for j in range(4):
        expo = jnp.exp(scores[j] - peak)
        total = total + jnp.sum(expo, axis=0, keepdims=True)
        acc = acc + dot(kvt[j][0], expo.astype(BF), 1, 0)
    mt_ref[pl.ds(pl.multiple_of(h * HD, HD), HD), :] = (acc[HD:] / total).astype(BF)
    lse_ref[0] = peak + jnp.log(total)


def attend(counts, qt, kv, kvt):
    heads = qt.shape[0]
    return pl.pallas_call(
        attend_kernel,
        out_shape=[jax.ShapeDtypeStruct((heads * HD, 512), BF), jax.ShapeDtypeStruct((heads, 1, 512), F32)],
        grid_spec=pltpu.PrefetchScalarGridSpec(
            num_scalar_prefetch=1,
            grid=(heads,),
            in_specs=[pl.BlockSpec((1, 128, 512), lambda h, c: (h, 0, 0))]
            + [pl.BlockSpec((1, 512, 128), lambda h, c: (h, 0, 0))] * 4
            + [pl.BlockSpec((1, 128, 512), lambda h, c: (h, 0, 0))] * 4,
            out_specs=[
                pl.BlockSpec((heads * HD, 512), lambda h, c: (0, 0)),
                pl.BlockSpec((1, 1, 512), lambda h, c: (h, 0, 0)),
            ],
        ),
        compiler_params=params(),
        cost_estimate=LIGHT,
        name="attend",
    )(counts, qt, *kv, *kvt)


def back_step(counts, qt, q, kv, kvt, dot_rows, lse, dkv_ref, fresh):
    dt = jnp.concatenate([jnp.zeros((HD, 512), BF), dot_rows], axis=0)
    d = dt.T
    probs, grads = [], []
    inner = jnp.zeros((1, 512), F32)
    for j in range(4):
        p = jnp.exp(masked(dot(kv[j][0], qt, 1, 0), counts[j]) - lse)
        g = dot(kv[j][0], dt, 1, 0)
        inner = inner + jnp.sum(p * g, axis=0, keepdims=True)
        probs.append(p)
        grads.append(g)
    dqt = jnp.zeros((128, 512), F32)
    for j in range(4):
        ds = (probs[j] * (grads[j] - inner)).astype(BF)
        dqt = dqt + dot(kvt[j][0], ds, 1, 0)
        dkv = dot(ds, q, 1, 0) + dot(probs[j].astype(BF), d, 1, 0)
        if fresh is None:
            dkv_ref[j] = dkv
        else:
            dkv_ref[j] = dkv_ref[j] + dkv
    return dqt[:HD] * 0.125


def back_own_kernel(counts, qt_ref, q_ref, *refs):
    kv, kvt, (dt_ref, lse_ref, dqt_ref, dkv_ref, bias_ref) = refs[:4], refs[4:8], refs[8:]
    dqt = back_step(counts, qt_ref[0], q_ref[0], kv, kvt, dt_ref[0], lse_ref[0], dkv_ref.at[0], None)
    dqt_ref[0] = dqt.astype(BF)
    bias_ref[0] = jnp.sum(dqt, axis=1, keepdims=True)


def back_own(counts, qt, q, kv, kvt, dt, lse):
    heads = qt.shape[0]
    tall, flat = pl.BlockSpec((1, 512, 128), lambda h, c: (h, 0, 0)), pl.BlockSpec((1, 128, 512), lambda h, c: (h, 0, 0))
    return pl.pallas_call(
        back_own_kernel,
        out_shape=[
            jax.ShapeDtypeStruct((heads, HD, 512), BF),
            jax.ShapeDtypeStruct((heads, 4, 512, 128), F32),
            jax.ShapeDtypeStruct((heads, HD, 1), F32),
        ],
        grid_spec=pltpu.PrefetchScalarGridSpec(
            num_scalar_prefetch=1,
            grid=(heads,),
            in_specs=[flat, tall]
            + [tall] * 4
            + [flat] * 4
            + [
                pl.BlockSpec((1, HD, 512), lambda h, c: (c[6], h, 0)),
                pl.BlockSpec((1, 1, 512), lambda h, c: (h, 0, 0)),
            ],
            out_specs=[
                pl.BlockSpec((1, HD, 512), lambda h, c: (h, 0, 0)),
                pl.BlockSpec((1, 4, 512, 128), lambda h, c: (h, 0, 0, 0)),
                pl.BlockSpec((1, HD, 1), lambda h, c: (h, 0, 0)),
            ],
        ),
        compiler_params=params(),
        cost_estimate=LIGHT,
        name="back_own",
    )(counts, qt, q, *kv, *kvt, dt, lse)


def back_head_kernel(few, apart, sc, *refs):
    qts, qs, kv, kvt = refs[:3], refs[3:6], refs[6:10], refs[10:14]
    ds, ls, (dq0_ref, dkv_ref, b_ref), xs = refs[14:17], refs[17:20], refs[20:23], refs[23:27]
    packet, outs, (acc, dqs, qb) = refs[27], refs[28:-3], refs[-3:]
    s = pl.program_id(0)

    @pl.when(s == 0)
    def _():
        acc[...] = dkv_ref[0]
        dqs[0] = dq0_ref[0]
        qb[...] = b_ref[0]

    choose = lambda a: jnp.where(s == 0, a[0], jnp.where(s == 1, a[1], a[2]))
    rows = choose([d[0] for d in ds])
    lse = choose([v[0] for v in ls])
    qt, q = choose([v[0] for v in qts]), choose([v[0] for v in qs])
    dqt = back_step(sc, qt, q, kv, kvt, rows, lse, acc, True)
    dqs[s + 1] = dqt.astype(BF)
    qb[...] += jnp.sum(dqt, axis=1, keepdims=True)

    @pl.when(s == 2)
    def _():
        dwt = jnp.zeros((256, 768), F32)
        vsum = jnp.zeros((1, 128), F32)
        for j in range(4):
            part = acc[j]
            vsum = vsum + jnp.sum(part, axis=0, keepdims=True)
            both = jnp.concatenate([dqs[j], part.astype(BF).T], axis=0)
            packet[jnp.bitwise_xor(sc[6], j)] = both
            both = jnp.concatenate([both, jnp.zeros((HD, 512), BF)], axis=0)
            dwt = dwt + dot(both, xs[j][...], 1, 0)
        lane = lax.broadcasted_iota(jnp.int32, (HD, 256), 1)
        vcol = jnp.broadcast_to(vsum, (128, 128)).T[HD:, :1]
        sums = jnp.where(lane == 192, qb[...], jnp.where(lane == 193, vcol, 0.0)).astype(BF)
        rows = 768 * few // HD
        dw = dwt.T + dot(spread(rows, few), sums, 1, 0)
        split_rows((sc[4], sc[5]), dw.astype(BF), outs[0], outs[1] if apart else None, 0)


def back_head(h, sc, qt, q, kv, kvt, dts, lses, dq0, dkv, bias0, xs, few):
    spec = pl.BlockSpec
    rows = 768 * few // HD
    apart = aligned(rows)
    tall, flat = spec((1, 512, 128), lambda s, c: (h, 0, 0)), spec((1, 128, 512), lambda s, c: (h, 0, 0))
    splits = split_shapes(apart, rows, 256)
    return pl.pallas_call(
        functools.partial(back_head_kernel, few, apart),
        out_shape=[jax.ShapeDtypeStruct((4, 3 * HD, 512), BF)] + splits,
        grid_spec=pltpu.PrefetchScalarGridSpec(
            num_scalar_prefetch=1,
            grid=(3,),
            in_specs=[flat] * 3
            + [tall] * 3
            + [tall] * 4
            + [flat] * 4
            + [spec((1, HD, 512), lambda s, c, j=j: (jnp.bitwise_xor(c[6], j), h, 0)) for j in (1, 2, 3)]
            + [spec((1, 1, 512), lambda s, c: (h, 0, 0))] * 3
            + [
                spec((1, HD, 512), lambda s, c: (h, 0, 0)),
                spec((1, 4, 512, 128), lambda s, c: (h, 0, 0, 0)),
                spec((1, HD, 1), lambda s, c: (h, 0, 0)),
            ]
            + [spec((512, 768), lambda s, c: (0, 0))] * 4,
            out_specs=[spec((4, 3 * HD, 512), lambda s, c: (0, 0, 0))]
            + [spec(v.shape, lambda s, c, d=len(v.shape): (0,) * d) for v in splits],
            scratch_shapes=[
                pltpu.VMEM((4, 512, 128), F32),
                pltpu.VMEM((4, HD, 512), BF),
                pltpu.VMEM((HD, 1), F32),
            ],
        ),
        compiler_params=params(),
        cost_estimate=pl.CostEstimate(flops=10**11, transcendentals=0, bytes_accessed=1),
        name="back_head",
    )(sc, *qt[1:], *q[1:], *kv, *kvt, *[dts] * 3, *lses, dq0, dkv, bias0, *xs)


def row_mean(v):
    return jnp.mean(v, axis=1, keepdims=True)


def norm(rows):
    center = rows - row_mean(rows)
    spread = lax.rsqrt(row_mean(center * center) + EPS)
    return center * spread, spread


def norm_back(grad, normed, spread, gain):
    scaled = grad * gain
    return spread * (scaled - row_mean(scaled) - normed * row_mean(scaled * normed))


def middle_kernel(few, sc, *refs):
    m0, m1, m2, m3, x_ref, cot_ref, vec_ref, weights = refs[:8]
    outer = refs[8:12]
    out_ref, g1_ref, d_ref = refs[12:15]
    dw_ref = refs[15]
    (wo_ref, n1_ref, s1_ref, hid_ref, hidb_ref, hidt_ref, acc_ref, gp_ref, act_ref, gsb_ref, gst_ref,
     dvec_ref, ib_ref, move_ref, part_ref, tail_ref, part_sem, tail_sem) = refs[16:]
    step = pl.program_id(0)
    vec = lambda i: vec_ref[pl.ds(i, 1), :]
    mixed = (m0, m1, m2, m3)
    inner = lambda: weights[:, 0, :, :768].reshape(768, 768)
    outer_full = lambda: weights[:, 0, :, 768:].reshape(768, 768)
    pad = jnp.zeros((64, 512), BF)
    own_rows = 768 * few // HD

    @pl.when(step == 0)
    def _():
        for k in range(4):
            wo_ref[:, k * 256 : k * 256 + 256] = outer[k][:, 0].reshape(768, 256)
        r, l = unit_index(0), unit_index(1)
        move_ref[...] = (r == (l % HD) // few * own_rows + (l % HD) % few).astype(F32).astype(BF)
        unit = lax.broadcasted_iota(jnp.int32, (128, 768), 0)
        lane = lax.broadcasted_iota(jnp.int32, (128, 768), 1)
        for k in range(4):
            spread = dot(wo_ref[:, k * 256 + 128 : k * 256 + 256], move_ref[...], 0, 0)
            ib_ref[k : k + 1] = jnp.sum(jnp.where(unit - 64 == lane // HD, spread, 0.0), axis=0, keepdims=True)
        rows = x_ref[...].astype(F32) + vec(0)
        for k in range(4):
            rows = rows + dot(mixed[k][...], wo_ref[:, k * 256 : k * 256 + 192], 0, 1)
        n1, s1 = norm(rows)
        hidden = n1 * vec(1) + vec(2)
        n1_ref[...] = n1
        s1_ref[...] = s1
        hid_ref[...] = hidden
        low = hidden.astype(BF)
        hidb_ref[...] = low
        hidt_ref[...] = low.T
        acc_ref[...] = hidden + vec(3)

    @pl.when(step < 4)
    def _():
        u = dot(hidb_ref[...], inner(), 1, 0) + ib_ref[pl.ds(step, 1), :]
        cdf = 0.5 + 0.5 * lax.erf(u * math.sqrt(0.5))
        act = (u * cdf).astype(BF)
        gp_ref[step] = cdf + u * jnp.exp(-0.5 * u * u) * (1.0 / math.sqrt(2.0 * math.pi))
        act_ref[step] = act
        acc_ref[...] += dot(act, outer_full(), 1, 1)

    @pl.when(step == 3)
    def _():
        valid = (lax.broadcasted_iota(jnp.int32, (512, 1), 0) < sc[0]).astype(F32)
        n2, s2 = norm(acc_ref[...])
        out_ref[...] = (valid * (n2 * vec(4) + vec(5))).astype(BF)
        g2 = cot_ref[...].astype(F32) * valid
        gs = norm_back(g2, n2, s2, vec(4))
        low = gs.astype(BF)
        gsb_ref[...] = low
        gst_ref[...] = low.T
        dvec_ref[pl.ds(3, 1), :] = jnp.sum(gs, axis=0, keepdims=True)
        dvec_ref[pl.ds(4, 1), :] = jnp.sum(g2 * n2, axis=0, keepdims=True)
        dvec_ref[pl.ds(5, 1), :] = jnp.sum(g2, axis=0, keepdims=True)
        acc_ref[...] = gs

    @pl.when(jnp.logical_and(step >= 4, step < 8))
    def _():
        k = 7 - step
        gi = dot(gsb_ref[...], outer_full(), 1, 0) * gp_ref[k]
        dvec_ref[pl.ds(8 + k, 1), :] = jnp.sum(gi, axis=0, keepdims=True)
        low = gi.astype(BF)
        acc_ref[...] += dot(low, inner(), 1, 1)
        turn = lax.rem(step, 2)
        leave = lambda k, turn: pltpu.make_async_copy(
            part_ref.at[turn], dw_ref.at[:, pl.ds(pl.multiple_of(k * 1792, 256), 1536)], part_sem.at[turn]
        )

        @pl.when(step >= 6)
        def _():
            leave(k + 2, turn).wait()

        part_ref[turn, :, :768] = dot(hidt_ref[...], low, 1, 0).astype(BF)
        part_ref[turn, :, 768:] = dot(gst_ref[...], act_ref[k], 1, 0).astype(BF)
        leave(k, turn).start()

    @pl.when(step == 8)
    def _():
        gh = acc_ref[...]
        n1 = n1_ref[...]
        g1 = norm_back(gh, n1, s1_ref[...], vec(1))
        g1_ref[...] = g1
        dvec_ref[pl.ds(0, 1), :] = jnp.sum(g1, axis=0, keepdims=True)
        dvec_ref[pl.ds(1, 1), :] = jnp.sum(gh * n1, axis=0, keepdims=True)
        dvec_ref[pl.ds(2, 1), :] = jnp.sum(gh, axis=0, keepdims=True)
        dvec_ref[pl.ds(6, 2), :] = jnp.zeros((2, 768), F32)
        dvec_ref[pl.ds(12, 4), :] = jnp.zeros((4, 768), F32)
        low = g1.astype(BF)
        lowt = low.T
        columns = dvec_ref[...].T
        lane = lax.broadcasted_iota(jnp.int32, (768, 256), 1)
        unit = lax.broadcasted_iota(jnp.int32, (768, 256), 0)
        shared = jnp.zeros((768, 256), F32)
        for v in range(6):
            shared = jnp.where(lane == 192 + v, columns[:, v : v + 1], shared)
        shared = shared.astype(BF).astype(F32)
        for k in range(4):
            d_ref[jnp.bitwise_xor(sc[6], k)] = dot(wo_ref[:, k * 256 : k * 256 + 192], lowt, 0, 0).astype(BF)
            full = jnp.concatenate([mixed[k][...], pad], axis=0)
            bias = jnp.where(lane - 200 == unit // HD, columns[:, 8 + k : 9 + k], 0.0).astype(BF)
            tail = dot(lowt, full, 1, 1) + shared + dot(move_ref[...], bias, 1, 0)
            tail_ref[k] = tail.astype(BF)
            pltpu.make_async_copy(
                tail_ref.at[k], dw_ref.at[:, k * 1792 + 1536 : k * 1792 + 1792], tail_sem.at[k]
            ).start()
        for k in range(4):
            pltpu.make_async_copy(
                tail_ref.at[k], dw_ref.at[:, k * 1792 + 1536 : k * 1792 + 1792], tail_sem.at[k]
            ).wait()
        for k in (1, 0):
            turn = (7 - k) % 2
            pltpu.make_async_copy(
                part_ref.at[turn], dw_ref.at[:, k * 1792 : k * 1792 + 1536], part_sem.at[turn]
            ).wait()


def unit_index(axis):
    return lax.broadcasted_iota(jnp.int32, (768, 768), axis)


def middle(sc, mixed, x, cot, vec, weights, few):
    spec = pl.BlockSpec
    fixed = lambda shape: spec(shape, lambda i, c: (0,) * len(shape))
    once = lambda shape: spec(shape, lambda i, c: (0,) * len(shape), pipeline_mode=pl.Buffered(1))
    shape = jax.ShapeDtypeStruct
    blocks, rows = weights.shape[0], weights.shape[2]
    turn = lambda i: jnp.where(i < 4, i, jnp.where(i < 8, 7 - i, 0))
    return pl.pallas_call(
        functools.partial(middle_kernel, few),
        out_shape=[shape((512, 768), BF), shape((512, 768), F32), shape((4, 192, 512), BF)]
        + [shape((768, 7168), BF)],
        grid_spec=pltpu.PrefetchScalarGridSpec(
            num_scalar_prefetch=1,
            grid=(9,),
            in_specs=[fixed((192, 512))] * 4
            + [fixed((512, 768)), fixed((512, 768)), fixed((8, 768))]
            + [spec((blocks, 1, rows, 1536), lambda i, c: (0, jnp.bitwise_xor(c[6], turn(i)), 0, 0))]
            + [spec((blocks, 1, rows, 256), lambda i, c, k=k: (0, jnp.bitwise_xor(c[6], k), 0, 6)) for k in range(4)],
            out_specs=[fixed((512, 768)), fixed((512, 768)), fixed((4, 192, 512))] + [spec(memory_space=pl.ANY)],
            scratch_shapes=[
                pltpu.VMEM((768, 1024), BF),
                pltpu.VMEM((512, 768), F32),
                pltpu.VMEM((512, 1), F32),
                pltpu.VMEM((512, 768), F32),
                pltpu.VMEM((512, 768), BF),
                pltpu.VMEM((768, 512), BF),
                pltpu.VMEM((512, 768), F32),
                pltpu.VMEM((4, 512, 768), F32),
                pltpu.VMEM((4, 512, 768), BF),
                pltpu.VMEM((512, 768), BF),
                pltpu.VMEM((768, 512), BF),
                pltpu.VMEM((16, 768), F32),
                pltpu.VMEM((8, 768), F32),
                pltpu.VMEM((768, 768), BF),
                pltpu.VMEM((2, 768, 1536), BF),
                pltpu.VMEM((4, 768, 256), BF),
                pltpu.SemaphoreType.DMA((2,)),
                pltpu.SemaphoreType.DMA((4,)),
            ],
        ),
        compiler_params=params(),
        cost_estimate=LIGHT,
        name="middle",
    )(sc, *mixed, x, cot, vec, *[weights] * 5)


def input_grad_kernel(heads, base_ref, w_ref, *refs):
    packets, (out, acc) = refs[:-2], refs[-2:]
    k = pl.program_id(0)

    @pl.when(k == 0)
    def _():
        acc[...] = jnp.zeros_like(acc)

    for packet, h in zip(packets, heads, strict=True):
        p = packet[0]
        p = jnp.concatenate([p[:HD], jnp.zeros((HD, 512), BF), p[HD:]], axis=0)
        acc[...] += dot(w_ref[:, 0, :, h * 256 : h * 256 + 256].reshape(768, 256), p, 1, 0)

    @pl.when(k == 3)
    def _():
        out[...] = base_ref[...] + acc[...].T


def input_grad(base, weights, packets, heads):
    blocks, _, rows, _ = weights.shape
    return pl.pallas_call(
        functools.partial(input_grad_kernel, heads),
        grid=(4,),
        out_shape=jax.ShapeDtypeStruct((512, 768), F32),
        in_specs=[whole((512, 768)), pl.BlockSpec((blocks, 1, rows, 768), lambda k: (0, k, 0, 0))]
        + [pl.BlockSpec((1, 192, 512), lambda k: (k, 0, 0))] * len(packets),
        out_specs=whole((512, 768)),
        scratch_shapes=[pltpu.VMEM((768, 512), F32)],
        compiler_params=params(),
        cost_estimate=LIGHT,
        name="input_grad",
    )(base, weights, *packets)


def body(
    tokens, cotangent, lengths, query_weight, key_weight, value_weight, query_bias, value_bias, output_weight,
    output_bias, first_gain, first_shift, inner_weight, inner_bias, outer_weight, outer_bias, second_gain, second_shift,
):
    n = lax.axis_size("dp")
    me = lax.axis_index("dp")
    rows = query_weight.shape[0]
    heads = query_weight.shape[1] // HD
    few, units = inner_bias.shape
    z = lax.axis_index("tensor")
    slots = jnp.arange(4) ^ z
    counts = jnp.clip(lengths[0] - slots * 512, 0, 512).astype(jnp.int32)
    place = jnp.stack([me & 1, me >> 1, z]).astype(jnp.int32)

    by_head = lambda w: w.reshape(rows, heads, HD)
    wide = jnp.stack(
        [by_head(query_weight), by_head(output_weight), by_head(key_weight), by_head(value_weight)], axis=2
    ).reshape(rows, heads * 256)
    small = jnp.stack([output_bias, first_gain, first_shift, outer_bias, second_gain, second_shift], axis=1)
    biases = jnp.pad(jnp.concatenate([query_bias, value_bias], axis=1), ((0, rows - few), (0, 0)))
    used = 6 + 2 * heads
    near = jnp.concatenate([wide, small, biases, jnp.zeros((rows, 128 - used), BF)], axis=1)

    extra = jnp.pad(inner_bias, ((0, rows - few), (0, 64 - units)))
    front = jnp.concatenate([inner_weight, outer_weight, output_weight, extra], axis=1)
    apart = aligned(rows)
    also = lambda a, m: jnp.concatenate([a, swap(a, "dp", m)], axis=0) if apart else a
    up, down = [tokens], [tokens]

    def hop():
        up.append(shift(up[-1], 1))
        down.append(shift(down[-1], -1))

    hop()
    near = also(near, 2)
    near, up[1], down[1], front = stage(near, up[1], down[1], front)
    front = gather_all(front)
    hop()
    near = also(near, 4)
    near, up[2], down[2], later = stage(near, up[2], down[2], wide)
    full = gather_all(later)
    hop()
    if apart:
        at = [me ^ m for m in (0, 2, 4, 6, 1, 3, 5, 7)]
        near, where = [near, swap(near, "dp", 1)], jnp.stack(at).astype(jnp.int32) * rows
    else:
        near, where = [gather_rows(near)], jnp.zeros((1,), jnp.int32)
    tile = assemble(near, where, 128, 6).astype(F32)
    vec = jnp.pad(tile[:, :6].T, ((0, 2), (0, 0)))
    tile = tile.reshape(n, rows, 128)[:, :few, 6:used].reshape(HD, used - 6).T
    blank = jnp.zeros((heads, 2 * HD), F32)
    bias = jnp.concatenate([tile[:heads], blank, tile[heads:]], axis=1)[:, None, :]
    xs = [by_slot(up, down, k) for k in range(3)]
    made = [project(x, (near, where), bias) for x in xs]
    made, up[3], down[3] = stage(made, up[3], down[3])
    xs.append(by_slot(up, down, 3))
    made.append(project(xs[3], (near, where), bias))
    qt, q, kv, kvt = ([m[i] for m in made] for i in range(4))

    mixed, lses = [None] * 4, [None] * 4
    for s in (3, 2, 1, 0):
        mixed[s], lses[s] = attend(counts, qt[s], kv, kvt)
        if s:
            come = mixed[s + 1] if s < 3 else ()
            mixed[s], qt[s - 1], come = stage(mixed[s], qt[s - 1], come)
            if s < 3:
                mixed[s + 1] = come
            mixed[s] = swap(mixed[s], "tensor", s)
    mixed, front = stage(mixed, front)

    sc = jnp.concatenate([counts, place])
    out, g1, d_out, dw = middle(sc, mixed, tokens, cotangent, vec, front, few)

    d = exchange(d_out)
    dq0, dkv, bias0 = back_own(sc, qt[0], q[0], kv, kvt, d_out, lses[0])
    dw, full, bias0 = stage(dw, full, bias0)
    total = lax.psum_scatter(dw, "dp", scatter_dimension=0, tiled=True)
    d, dq0, dkv, bias0 = stage(d, dq0, dkv, bias0)
    head = lambda h, d: back_head(h, sc, qt, q, kv, kvt, d, lses[1:], dq0, dkv, bias0, xs, few)
    packet0, *dw0 = head(0, d)
    packet0, dw0, d = stage(packet0, dw0, d)
    packet0 = exchange(packet0)
    packet1, *dw1 = head(1, d)
    packet0, packet1, dw1, d = stage(packet0, packet1, dw1, d)
    packet1 = exchange(packet1)
    packet2, *dw2 = head(2, d)
    packet1, packet2, dw2 = stage(packet1, packet2, dw2)

    packet2 = exchange(packet2)
    dws = [dw0, dw1, dw2]
    joined = lambda arrays: jnp.concatenate(arrays, axis=-1)
    if apart:
        keep, got = joined([v[0] for v in dws]), swap(joined([v[1] for v in dws]), "dp", 1)
        block = lambda m: keep[m].astype(F32) + got[m].astype(F32)
        passed = swap(jnp.stack([block(1), block(3)]).astype(BF), "dp", 2)
        near_by = (block(2) + passed[1].astype(F32)).astype(BF)
        own = block(0) + passed[0].astype(F32)
    else:
        own, near_by = joined([v[0] for v in dws]), ()
    ahead = input_grad(g1, full, [packet0, packet1], (0, 1))
    ahead, own, near_by, total = stage(ahead, own, near_by, total)
    slots = [total[:, k * 1792 : k * 1792 + 1792] for k in range(4)]
    moved = [swap(v, "tensor", k) for k, v in enumerate(slots) if k]
    own = own + swap(near_by, "dp", 4).astype(F32) if apart else sum_rows(own)
    tokens_grad = input_grad(ahead, full, [packet2], (2,))
    side = lambda i: jnp.concatenate([own[:, h * 256 + i * HD : h * 256 + i * HD + HD] for h in range(heads)], axis=1)
    sides = [side(i) for i in range(3)]
    qb = jnp.stack([own[:few, h * 256 + 192] for h in range(heads)], axis=1)
    vb = jnp.stack([own[:few, h * 256 + 193] for h in range(heads)], axis=1)
    tokens_grad, sides, qb, vb, moved = stage(tokens_grad, sides, qb, vb, moved)

    sums = (slots[0].astype(F32) + moved[0].astype(F32)) + (moved[1].astype(F32) + moved[2].astype(F32))
    ffn, rest = sums[:, :1536], sums[:, 1536:]
    return (
        out,
        tokens_grad,
        *sides,
        qb,
        vb,
        rest[:, :192],
        rest[:, 192],
        rest[:, 193],
        rest[:, 194],
        ffn[:, :768],
        rest[:few, 200 : 200 + units],
        ffn[:, 768:],
        rest[:, 195],
        rest[:, 196],
        rest[:, 197],
    )


def solution(mesh):
    table, vector, token = P("dp", "tensor"), P("dp"), P(("dp", "tensor"), None)
    return jax.shard_map(
        body,
        mesh=mesh,
        in_specs=(
            token, token, vector, table, table, table, table, table, table,
            vector, vector, vector, table, table, table, vector, vector, vector,
        ),
        out_specs=(
            token, token, table, table, table, table, table, table,
            vector, vector, vector, table, table, table, vector, vector, vector,
        ),
        check_vma=False,
    )
```

```python
import functools
import math

import jax
import jax.numpy as jnp
from jax import lax
from jax.experimental import pallas as pl
from jax.experimental.pallas import tpu as pltpu
from jax.sharding import PartitionSpec as P

HD = 64
SLOT_LEN = 2048
EPS = 1e-05
NEG = -1e30
BF = jnp.bfloat16
F32 = jnp.float32
VMEM_LIMIT = 60 * 1024 * 1024
LIGHT = pl.CostEstimate(flops=1, transcendentals=0, bytes_accessed=1)


def dot(a, b, ca, cb):
    return lax.dot_general(a, b, (((ca,), (cb,)), ((), ())), preferred_element_type=F32)


def whole(shape):
    return pl.BlockSpec(shape, lambda *_: (0,) * len(shape))


def params():
    return pltpu.CompilerParams(vmem_limit_bytes=VMEM_LIMIT)


def swap(x, axis, mask):
    n = lax.axis_size(axis)
    return lax.ppermute(x, axis, [(i, i ^ mask) for i in range(n)])


def dp_groups():
    n, bit, groups = lax.axis_size("dp"), 2, []
    while bit < n:
        if bit * 2 < n:
            groups.append((bit, bit * 2, bit * 3))
            bit *= 4
        else:
            groups.append((bit,))
            bit *= 2
    return groups


def stage(*values):
    return lax.optimization_barrier(values)


def shift(x, by):
    n = lax.axis_size("tensor")
    return lax.ppermute(x, "tensor", [(i, i + by) for i in range(n) if 0 <= i + by < n])


def by_slot(up, down, k):
    z = lax.axis_index("tensor")
    odd, high = z % 2 == 1, z >= 2
    if k == 0:
        return up[0]
    if k == 1:
        return jnp.where(odd, up[1], down[1])
    if k == 2:
        return jnp.where(high, up[2], down[2])
    return jnp.where(odd, jnp.where(high, up[3], down[1]), jnp.where(high, up[1], down[3]))


def exchange(blocks):
    return lax.all_to_all(blocks, "tensor", 0, 0)


def aligned(rows):
    return rows % 16 == 0 and lax.axis_size("dp") == 8


def gather_all(piece):
    n, t = lax.axis_size("dp"), lax.axis_size("tensor")
    rows, cols = piece.shape
    blocks = lax.all_gather(piece, ("dp", "tensor")).reshape(n, t, rows, cols)
    if aligned(rows):
        return blocks
    return blocks.transpose(1, 0, 2, 3).reshape(1, t, n * rows, cols)


def gather_rows(piece):
    rows, cols = piece.shape
    n = lax.axis_size("dp")
    me = lax.axis_index("dp")
    pieces = [((0,), piece)]
    for group in dp_groups():
        if len(pieces) > 1:
            pieces = [(sum((m for m, _ in pieces), ()), jnp.concatenate([a for _, a in pieces], axis=0))]
        masks, array = pieces[0]
        pieces += [(tuple(m ^ g for m in masks), swap(array, "dp", g)) for g in group]
    pieces += [(tuple(m ^ 1 for m in masks), swap(array, "dp", 1)) for masks, array in pieces]
    order = [m for masks, _ in pieces for m in masks]
    place = [order.index(m) for m in range(n)]
    stacked = jnp.concatenate([a for _, a in pieces], axis=0).reshape(n, rows, cols)
    index = jnp.take(jnp.array(place, jnp.int32), me ^ jnp.arange(n))
    return jnp.take(stacked, index, axis=0).reshape(n * rows, cols)


def put(where, refs, out):
    if len(refs) == 1:
        out[...] = refs[0][...]
        return
    count = out.shape[0] // refs[0].shape[0]
    each = (where.shape[0] if hasattr(where, "shape") else len(where)) // count
    rows = refs[0].shape[0] // each
    for s, ref in enumerate(refs):
        for b in range(each):
            out[pl.ds(pl.multiple_of(where[each * s + b], rows), rows), :] = ref[b * rows : (b + 1) * rows]


def assemble_kernel(where, *refs):
    put(where, refs[:-1], refs[-1])


def assemble(pieces, where, block, at):
    rows, n = pieces[0].shape[0], len(pieces)
    return pl.pallas_call(
        assemble_kernel,
        out_shape=jax.ShapeDtypeStruct((n * rows, block), pieces[0].dtype),
        grid_spec=pltpu.PrefetchScalarGridSpec(
            num_scalar_prefetch=1,
            grid=(1,),
            in_specs=[pl.BlockSpec((rows, block), lambda i, w: (0, at))] * n,
            out_specs=pl.BlockSpec((n * rows, block), lambda i, w: (0, 0)),
        ),
        compiler_params=params(),
        cost_estimate=LIGHT,
        name="assemble",
    )(where, *pieces)


def split_rows(place, value, keep, send, lane):
    lanes = slice(lane, lane + value.shape[1])
    if send is None:
        keep[:, lanes] = value
        return
    rows = keep.shape[1]
    for j in range(4):
        at = jnp.bitwise_xor(j, place[1])
        even, odd = value[2 * j * rows : (2 * j + 1) * rows], value[(2 * j + 1) * rows : (2 * j + 2) * rows]
        keep[at, :, lanes] = jnp.where(place[0] == 0, even, odd)
        send[at, :, lanes] = jnp.where(place[0] == 0, odd, even)


def add_kernel(groups, *refs):
    outs = refs[len(refs) - len(groups) :]
    for out, terms in zip(outs, groups, strict=True):
        total = refs[terms[0]][...].astype(F32)
        for t in terms[1:]:
            total = total + refs[t][...].astype(F32)
        out[...] = total.reshape(out.shape).astype(out.dtype)


def add(terms, outs):
    lanes = outs[0][1]
    block = 1792
    specs = []
    for array, lead, start in terms:
        rows = array.shape[-2]
        if lead is None:
            specs.append(pl.BlockSpec((rows, block), lambda i, s=start // block: (0, i + s)))
        else:
            specs.append(pl.BlockSpec((1, rows, block), lambda i, m=lead, s=start // block: (m, 0, i + s)))
    rows = terms[0][0].shape[-2]
    return pl.pallas_call(
        functools.partial(add_kernel, [numbers for numbers, _, _ in outs]),
        grid=(lanes // block,),
        out_shape=[jax.ShapeDtypeStruct((rows, lanes), d) for _, _, d in outs],
        in_specs=specs,
        out_specs=[pl.BlockSpec((rows, block), lambda i: (0, i))] * len(outs),
        compiler_params=params(),
        cost_estimate=LIGHT,
        name="add",
    )(*[a for a, _, _ in terms])


def sum_rows(array):
    n = lax.axis_size("dp")
    me = lax.axis_index("dp")
    halves = array.reshape(n // 2, 2, array.shape[0] // n, array.shape[1])
    side = lambda c: lax.dynamic_index_in_dim(halves, c, 1, keepdims=False)
    total = side(me & 1).astype(F32) + swap(side(1 - (me & 1)), "dp", 1).astype(F32)
    for group in reversed(dp_groups()):
        count = len(group) + 1
        total = total.reshape(count, -1, *total.shape[1:])
        mine = (me // group[0]) % count
        sent = total.astype(BF)
        terms = [swap(pick(sent, mine ^ (g // group[0])), "dp", g).astype(F32) for g in group]
        total = pick(total, mine)
        for t in terms:
            total = total + t
    return total.reshape(total.shape[-2:])


def pick(array, index):
    return lax.dynamic_index_in_dim(array, index, 0, keepdims=False)


def split_shapes(aligned_rows, rows, cols):
    shape = jax.ShapeDtypeStruct
    return [shape((4, rows, cols), BF)] * 2 if aligned_rows else [shape((768, cols), BF)]


def spread(rows, few):
    i = lax.broadcasted_iota(jnp.int32, (768, HD), 1)
    r = lax.broadcasted_iota(jnp.int32, (768, HD), 0)
    return (r == (i // few) * rows + i % few).astype(F32).astype(BF)


def project_kernel(where, x_ref, b_ref, *refs):
    pieces, (qt_ref, q_ref, kv_ref, kvt_ref, w) = refs[:-5], refs[-5:]
    put(where, pieces, w)
    y = dot(x_ref[...], w[...], 1, 0) + b_ref[0]
    keep = lax.broadcasted_iota(jnp.int32, (512, 128), 1) < HD
    q = jnp.where(keep, y[:, :128].astype(BF).astype(F32) * 0.125, 0.0).astype(BF)
    kv = y[:, 128:].astype(BF)
    q_ref[0] = q
    qt_ref[0] = q.T
    kv_ref[0] = kv
    kvt_ref[0] = kv.T


def project(x, near, bias):
    pieces, where = near
    heads, rows = bias.shape[0], pieces[0].shape[0]
    shapes = [(heads, 128, 512), (heads, 512, 128), (heads, 512, 128), (heads, 128, 512)]
    return pl.pallas_call(
        project_kernel,
        out_shape=[jax.ShapeDtypeStruct(s, BF) for s in shapes],
        grid_spec=pltpu.PrefetchScalarGridSpec(
            num_scalar_prefetch=1,
            grid=(heads,),
            in_specs=[whole((512, 768)), pl.BlockSpec((1, 1, 256), lambda h, w: (h, 0, 0))]
            + [pl.BlockSpec((rows, 256), lambda h, w: (0, h))] * len(pieces),
            out_specs=[pl.BlockSpec((1, *s[1:]), lambda h, w: (h, 0, 0)) for s in shapes],
            scratch_shapes=[pltpu.VMEM((768, 256), BF)],
        ),
        compiler_params=params(),
        cost_estimate=LIGHT,
        name="project",
    )(where, x, bias, *pieces)


def masked(scores, count):
    return jnp.where(lax.broadcasted_iota(jnp.int32, scores.shape, 0) < count, scores, NEG)


def attend_kernel(counts, qt_ref, k0, k1, k2, k3, t0, t1, t2, t3, mt_ref, lse_ref):
    h = pl.program_id(0)
    qt = qt_ref[0]
    kvt = (t0, t1, t2, t3)
    scores = [masked(dot(k[0], qt, 1, 0), counts[j]) for j, k in enumerate((k0, k1, k2, k3))]
    peak = functools.reduce(jnp.maximum, [jnp.max(s, axis=0, keepdims=True) for s in scores])
    total = jnp.zeros((1, 512), F32)
    acc = jnp.zeros((128, 512), F32)
    for j in range(4):
        expo = jnp.exp(scores[j] - peak)
        total = total + jnp.sum(expo, axis=0, keepdims=True)
        acc = acc + dot(kvt[j][0], expo.astype(BF), 1, 0)
    mt_ref[pl.ds(pl.multiple_of(h * HD, HD), HD), :] = (acc[HD:] / total).astype(BF)
    lse_ref[0] = peak + jnp.log(total)


def attend(counts, qt, kv, kvt):
    heads = qt.shape[0]
    return pl.pallas_call(
        attend_kernel,
        out_shape=[jax.ShapeDtypeStruct((heads * HD, 512), BF), jax.ShapeDtypeStruct((heads, 1, 512), F32)],
        grid_spec=pltpu.PrefetchScalarGridSpec(
            num_scalar_prefetch=1,
            grid=(heads,),
            in_specs=[pl.BlockSpec((1, 128, 512), lambda h, c: (h, 0, 0))]
            + [pl.BlockSpec((1, 512, 128), lambda h, c: (h, 0, 0))] * 4
            + [pl.BlockSpec((1, 128, 512), lambda h, c: (h, 0, 0))] * 4,
            out_specs=[
                pl.BlockSpec((heads * HD, 512), lambda h, c: (0, 0)),
                pl.BlockSpec((1, 1, 512), lambda h, c: (h, 0, 0)),
            ],
        ),
        compiler_params=params(),
        cost_estimate=LIGHT,
        name="attend",
    )(counts, qt, *kv, *kvt)


def back_step(counts, qt, q, kv, kvt, dot_rows, lse, dkv_ref, fresh):
    dt = jnp.concatenate([jnp.zeros((HD, 512), BF), dot_rows], axis=0)
    d = dt.T
    probs, grads = [], []
    inner = jnp.zeros((1, 512), F32)
    for j in range(4):
        p = jnp.exp(masked(dot(kv[j][0], qt, 1, 0), counts[j]) - lse)
        g = dot(kv[j][0], dt, 1, 0)
        inner = inner + jnp.sum(p * g, axis=0, keepdims=True)
        probs.append(p)
        grads.append(g)
    dqt = jnp.zeros((128, 512), F32)
    for j in range(4):
        ds = (probs[j] * (grads[j] - inner)).astype(BF)
        dqt = dqt + dot(kvt[j][0], ds, 1, 0)
        dkv = dot(ds, q, 1, 0) + dot(probs[j].astype(BF), d, 1, 0)
        if fresh is None:
            dkv_ref[j] = dkv
        else:
            dkv_ref[j] = dkv_ref[j] + dkv
    return dqt[:HD] * 0.125


def back_own_kernel(counts, qt_ref, q_ref, *refs):
    kv, kvt, (dt_ref, lse_ref, dqt_ref, dkv_ref, bias_ref) = refs[:4], refs[4:8], refs[8:]
    dqt = back_step(counts, qt_ref[0], q_ref[0], kv, kvt, dt_ref[0], lse_ref[0], dkv_ref.at[0], None)
    dqt_ref[0] = dqt.astype(BF)
    bias_ref[0] = jnp.sum(dqt, axis=1, keepdims=True)


def back_own(counts, qt, q, kv, kvt, dt, lse):
    heads = qt.shape[0]
    tall, flat = pl.BlockSpec((1, 512, 128), lambda h, c: (h, 0, 0)), pl.BlockSpec((1, 128, 512), lambda h, c: (h, 0, 0))
    return pl.pallas_call(
        back_own_kernel,
        out_shape=[
            jax.ShapeDtypeStruct((heads, HD, 512), BF),
            jax.ShapeDtypeStruct((heads, 4, 512, 128), F32),
            jax.ShapeDtypeStruct((heads, HD, 1), F32),
        ],
        grid_spec=pltpu.PrefetchScalarGridSpec(
            num_scalar_prefetch=1,
            grid=(heads,),
            in_specs=[flat, tall]
            + [tall] * 4
            + [flat] * 4
            + [
                pl.BlockSpec((1, HD, 512), lambda h, c: (c[6], h, 0)),
                pl.BlockSpec((1, 1, 512), lambda h, c: (h, 0, 0)),
            ],
            out_specs=[
                pl.BlockSpec((1, HD, 512), lambda h, c: (h, 0, 0)),
                pl.BlockSpec((1, 4, 512, 128), lambda h, c: (h, 0, 0, 0)),
                pl.BlockSpec((1, HD, 1), lambda h, c: (h, 0, 0)),
            ],
        ),
        compiler_params=params(),
        cost_estimate=LIGHT,
        name="back_own",
    )(counts, qt, q, *kv, *kvt, dt, lse)


def back_head_kernel(few, apart, sc, *refs):
    qts, qs, kv, kvt = refs[:3], refs[3:6], refs[6:10], refs[10:14]
    ds, ls, (dq0_ref, dkv_ref, b_ref), xs = refs[14:17], refs[17:20], refs[20:23], refs[23:27]
    packet, outs, (acc, dqs, qb) = refs[27], refs[28:-3], refs[-3:]
    s = pl.program_id(0)

    @pl.when(s == 0)
    def _():
        acc[...] = dkv_ref[0]
        dqs[0] = dq0_ref[0]
        qb[...] = b_ref[0]

    choose = lambda a: jnp.where(s == 0, a[0], jnp.where(s == 1, a[1], a[2]))
    rows = choose([d[0] for d in ds])
    lse = choose([v[0] for v in ls])
    qt, q = choose([v[0] for v in qts]), choose([v[0] for v in qs])
    dqt = back_step(sc, qt, q, kv, kvt, rows, lse, acc, True)
    dqs[s + 1] = dqt.astype(BF)
    qb[...] += jnp.sum(dqt, axis=1, keepdims=True)

    @pl.when(s == 2)
    def _():
        dwt = jnp.zeros((256, 768), F32)
        vsum = jnp.zeros((1, 128), F32)
        for j in range(4):
            part = acc[j]
            vsum = vsum + jnp.sum(part, axis=0, keepdims=True)
            both = jnp.concatenate([dqs[j], part.astype(BF).T], axis=0)
            packet[jnp.bitwise_xor(sc[6], j)] = both
            both = jnp.concatenate([both, jnp.zeros((HD, 512), BF)], axis=0)
            dwt = dwt + dot(both, xs[j][...], 1, 0)
        lane = lax.broadcasted_iota(jnp.int32, (HD, 256), 1)
        vcol = jnp.broadcast_to(vsum, (128, 128)).T[HD:, :1]
        sums = jnp.where(lane == 192, qb[...], jnp.where(lane == 193, vcol, 0.0)).astype(BF)
        rows = 768 * few // HD
        dw = dwt.T + dot(spread(rows, few), sums, 1, 0)
        split_rows((sc[4], sc[5]), dw.astype(BF), outs[0], outs[1] if apart else None, 0)


def back_head(h, sc, qt, q, kv, kvt, dts, lses, dq0, dkv, bias0, xs, few):
    spec = pl.BlockSpec
    rows = 768 * few // HD
    apart = aligned(rows)
    tall, flat = spec((1, 512, 128), lambda s, c: (h, 0, 0)), spec((1, 128, 512), lambda s, c: (h, 0, 0))
    splits = split_shapes(apart, rows, 256)
    return pl.pallas_call(
        functools.partial(back_head_kernel, few, apart),
        out_shape=[jax.ShapeDtypeStruct((4, 3 * HD, 512), BF)] + splits,
        grid_spec=pltpu.PrefetchScalarGridSpec(
            num_scalar_prefetch=1,
            grid=(3,),
            in_specs=[flat] * 3
            + [tall] * 3
            + [tall] * 4
            + [flat] * 4
            + [spec((1, HD, 512), lambda s, c, j=j: (jnp.bitwise_xor(c[6], j), h, 0)) for j in (1, 2, 3)]
            + [spec((1, 1, 512), lambda s, c: (h, 0, 0))] * 3
            + [
                spec((1, HD, 512), lambda s, c: (h, 0, 0)),
                spec((1, 4, 512, 128), lambda s, c: (h, 0, 0, 0)),
                spec((1, HD, 1), lambda s, c: (h, 0, 0)),
            ]
            + [spec((512, 768), lambda s, c: (0, 0))] * 4,
            out_specs=[spec((4, 3 * HD, 512), lambda s, c: (0, 0, 0))]
            + [spec(v.shape, lambda s, c, d=len(v.shape): (0,) * d) for v in splits],
            scratch_shapes=[
                pltpu.VMEM((4, 512, 128), F32),
                pltpu.VMEM((4, HD, 512), BF),
                pltpu.VMEM((HD, 1), F32),
            ],
        ),
        compiler_params=params(),
        cost_estimate=pl.CostEstimate(flops=10**11, transcendentals=0, bytes_accessed=1),
        name="back_head",
    )(sc, *qt[1:], *q[1:], *kv, *kvt, *[dts] * 3, *lses, dq0, dkv, bias0, *xs)


def row_mean(v):
    return jnp.mean(v, axis=1, keepdims=True)


def norm(rows):
    center = rows - row_mean(rows)
    spread = lax.rsqrt(row_mean(center * center) + EPS)
    return center * spread, spread


def norm_back(grad, normed, spread, gain):
    scaled = grad * gain
    return spread * (scaled - row_mean(scaled) - normed * row_mean(scaled * normed))


def middle_kernel(few, sc, *refs):
    m0, m1, m2, m3, x_ref, cot_ref, vec_ref, weights = refs[:8]
    outer = refs[8:12]
    out_ref, g1_ref, d_ref = refs[12:15]
    dw_ref = refs[15]
    (wo_ref, n1_ref, s1_ref, hid_ref, hidb_ref, hidt_ref, acc_ref, gp_ref, act_ref, gsb_ref, gst_ref,
     dvec_ref, ib_ref, move_ref, part_ref, tail_ref, part_sem, tail_sem) = refs[16:]
    step = pl.program_id(0)
    vec = lambda i: vec_ref[pl.ds(i, 1), :]
    mixed = (m0, m1, m2, m3)
    inner = lambda: weights[:, 0, :, :768].reshape(768, 768)
    outer_full = lambda: weights[:, 0, :, 768:].reshape(768, 768)
    pad = jnp.zeros((64, 512), BF)
    own_rows = 768 * few // HD

    @pl.when(step == 0)
    def _():
        for k in range(4):
            wo_ref[:, k * 256 : k * 256 + 256] = outer[k][:, 0].reshape(768, 256)
        r, l = unit_index(0), unit_index(1)
        move_ref[...] = (r == (l % HD) // few * own_rows + (l % HD) % few).astype(F32).astype(BF)
        unit = lax.broadcasted_iota(jnp.int32, (128, 768), 0)
        lane = lax.broadcasted_iota(jnp.int32, (128, 768), 1)
        for k in range(4):
            spread = dot(wo_ref[:, k * 256 + 128 : k * 256 + 256], move_ref[...], 0, 0)
            ib_ref[k : k + 1] = jnp.sum(jnp.where(unit - 64 == lane // HD, spread, 0.0), axis=0, keepdims=True)
        rows = x_ref[...].astype(F32) + vec(0)
        for k in range(4):
            rows = rows + dot(mixed[k][...], wo_ref[:, k * 256 : k * 256 + 192], 0, 1)
        n1, s1 = norm(rows)
        hidden = n1 * vec(1) + vec(2)
        n1_ref[...] = n1
        s1_ref[...] = s1
        hid_ref[...] = hidden
        low = hidden.astype(BF)
        hidb_ref[...] = low
        hidt_ref[...] = low.T
        acc_ref[...] = hidden + vec(3)

    @pl.when(step < 4)
    def _():
        u = dot(hidb_ref[...], inner(), 1, 0) + ib_ref[pl.ds(step, 1), :]
        cdf = 0.5 + 0.5 * lax.erf(u * math.sqrt(0.5))
        act = (u * cdf).astype(BF)
        gp_ref[step] = cdf + u * jnp.exp(-0.5 * u * u) * (1.0 / math.sqrt(2.0 * math.pi))
        act_ref[step] = act
        acc_ref[...] += dot(act, outer_full(), 1, 1)

    @pl.when(step == 3)
    def _():
        valid = (lax.broadcasted_iota(jnp.int32, (512, 1), 0) < sc[0]).astype(F32)
        n2, s2 = norm(acc_ref[...])
        out_ref[...] = (valid * (n2 * vec(4) + vec(5))).astype(BF)
        g2 = cot_ref[...].astype(F32) * valid
        gs = norm_back(g2, n2, s2, vec(4))
        low = gs.astype(BF)
        gsb_ref[...] = low
        gst_ref[...] = low.T
        dvec_ref[pl.ds(3, 1), :] = jnp.sum(gs, axis=0, keepdims=True)
        dvec_ref[pl.ds(4, 1), :] = jnp.sum(g2 * n2, axis=0, keepdims=True)
        dvec_ref[pl.ds(5, 1), :] = jnp.sum(g2, axis=0, keepdims=True)
        acc_ref[...] = gs

    @pl.when(jnp.logical_and(step >= 4, step < 8))
    def _():
        k = 7 - step
        gi = dot(gsb_ref[...], outer_full(), 1, 0) * gp_ref[k]
        dvec_ref[pl.ds(8 + k, 1), :] = jnp.sum(gi, axis=0, keepdims=True)
        low = gi.astype(BF)
        acc_ref[...] += dot(low, inner(), 1, 1)
        turn = lax.rem(step, 2)
        leave = lambda k, turn: pltpu.make_async_copy(
            part_ref.at[turn], dw_ref.at[:, pl.ds(pl.multiple_of(k * 1792, 256), 1536)], part_sem.at[turn]
        )

        @pl.when(step >= 6)
        def _():
            leave(k + 2, turn).wait()

        part_ref[turn, :, :768] = dot(hidt_ref[...], low, 1, 0).astype(BF)
        part_ref[turn, :, 768:] = dot(gst_ref[...], act_ref[k], 1, 0).astype(BF)
        leave(k, turn).start()

    @pl.when(step == 8)
    def _():
        gh = acc_ref[...]
        n1 = n1_ref[...]
        g1 = norm_back(gh, n1, s1_ref[...], vec(1))
        g1_ref[...] = g1
        dvec_ref[pl.ds(0, 1), :] = jnp.sum(g1, axis=0, keepdims=True)
        dvec_ref[pl.ds(1, 1), :] = jnp.sum(gh * n1, axis=0, keepdims=True)
        dvec_ref[pl.ds(2, 1), :] = jnp.sum(gh, axis=0, keepdims=True)
        dvec_ref[pl.ds(6, 2), :] = jnp.zeros((2, 768), F32)
        dvec_ref[pl.ds(12, 4), :] = jnp.zeros((4, 768), F32)
        low = g1.astype(BF)
        lowt = low.T
        columns = dvec_ref[...].T
        lane = lax.broadcasted_iota(jnp.int32, (768, 256), 1)
        unit = lax.broadcasted_iota(jnp.int32, (768, 256), 0)
        shared = jnp.zeros((768, 256), F32)
        for v in range(6):
            shared = jnp.where(lane == 192 + v, columns[:, v : v + 1], shared)
        shared = shared.astype(BF).astype(F32)
        for k in range(4):
            d_ref[jnp.bitwise_xor(sc[6], k)] = dot(wo_ref[:, k * 256 : k * 256 + 192], lowt, 0, 0).astype(BF)
            full = jnp.concatenate([mixed[k][...], pad], axis=0)
            bias = jnp.where(lane - 200 == unit // HD, columns[:, 8 + k : 9 + k], 0.0).astype(BF)
            tail = dot(lowt, full, 1, 1) + shared + dot(move_ref[...], bias, 1, 0)
            tail_ref[k] = tail.astype(BF)
            pltpu.make_async_copy(
                tail_ref.at[k], dw_ref.at[:, k * 1792 + 1536 : k * 1792 + 1792], tail_sem.at[k]
            ).start()
        for k in range(4):
            pltpu.make_async_copy(
                tail_ref.at[k], dw_ref.at[:, k * 1792 + 1536 : k * 1792 + 1792], tail_sem.at[k]
            ).wait()
        for k in (1, 0):
            turn = (7 - k) % 2
            pltpu.make_async_copy(
                part_ref.at[turn], dw_ref.at[:, k * 1792 : k * 1792 + 1536], part_sem.at[turn]
            ).wait()


def unit_index(axis):
    return lax.broadcasted_iota(jnp.int32, (768, 768), axis)


def middle(sc, mixed, x, cot, vec, weights, few):
    spec = pl.BlockSpec
    fixed = lambda shape: spec(shape, lambda i, c: (0,) * len(shape))
    once = lambda shape: spec(shape, lambda i, c: (0,) * len(shape), pipeline_mode=pl.Buffered(1))
    shape = jax.ShapeDtypeStruct
    blocks, rows = weights.shape[0], weights.shape[2]
    turn = lambda i: jnp.where(i < 4, i, jnp.where(i < 8, 7 - i, 0))
    return pl.pallas_call(
        functools.partial(middle_kernel, few),
        out_shape=[shape((512, 768), BF), shape((512, 768), F32), shape((4, 192, 512), BF)]
        + [shape((768, 7168), BF)],
        grid_spec=pltpu.PrefetchScalarGridSpec(
            num_scalar_prefetch=1,
            grid=(9,),
            in_specs=[fixed((192, 512))] * 4
            + [fixed((512, 768)), fixed((512, 768)), fixed((8, 768))]
            + [spec((blocks, 1, rows, 1536), lambda i, c: (0, jnp.bitwise_xor(c[6], turn(i)), 0, 0))]
            + [spec((blocks, 1, rows, 256), lambda i, c, k=k: (0, jnp.bitwise_xor(c[6], k), 0, 6)) for k in range(4)],
            out_specs=[fixed((512, 768)), fixed((512, 768)), fixed((4, 192, 512))] + [spec(memory_space=pl.ANY)],
            scratch_shapes=[
                pltpu.VMEM((768, 1024), BF),
                pltpu.VMEM((512, 768), F32),
                pltpu.VMEM((512, 1), F32),
                pltpu.VMEM((512, 768), F32),
                pltpu.VMEM((512, 768), BF),
                pltpu.VMEM((768, 512), BF),
                pltpu.VMEM((512, 768), F32),
                pltpu.VMEM((4, 512, 768), F32),
                pltpu.VMEM((4, 512, 768), BF),
                pltpu.VMEM((512, 768), BF),
                pltpu.VMEM((768, 512), BF),
                pltpu.VMEM((16, 768), F32),
                pltpu.VMEM((8, 768), F32),
                pltpu.VMEM((768, 768), BF),
                pltpu.VMEM((2, 768, 1536), BF),
                pltpu.VMEM((4, 768, 256), BF),
                pltpu.SemaphoreType.DMA((2,)),
                pltpu.SemaphoreType.DMA((4,)),
            ],
        ),
        compiler_params=params(),
        cost_estimate=LIGHT,
        name="middle",
    )(sc, *mixed, x, cot, vec, *[weights] * 5)


def input_grad_kernel(heads, base_ref, w_ref, *refs):
    packets, (out, acc) = refs[:-2], refs[-2:]
    k = pl.program_id(0)

    @pl.when(k == 0)
    def _():
        acc[...] = jnp.zeros_like(acc)

    blank = jnp.zeros((HD, 512), BF)
    rows = {(i, h): p[0, i * HD : i * HD + HD] for p, h in zip(packets, heads, strict=True) for i in range(3)}
    for b in range(5):
        pair = [rows.get((v // 3, v % 3)) for v in (2 * b, 2 * b + 1)]
        if any(v is not None for v in pair):
            p = jnp.concatenate([blank if v is None else v for v in pair], axis=0)
            acc[...] += dot(w_ref[:, 0, :, b * 128 : b * 128 + 128].reshape(768, 128), p, 1, 0)

    @pl.when(k == 3)
    def _():
        out[...] = base_ref[...] + acc[...].T


def input_grad(base, weights, packets, heads):
    blocks, _, rows, _ = weights.shape
    return pl.pallas_call(
        functools.partial(input_grad_kernel, heads),
        out_shape=jax.ShapeDtypeStruct((512, 768), F32),
        grid=(4,),
        in_specs=[whole((512, 768)), pl.BlockSpec((blocks, 1, rows, 640), lambda k: (0, k, 0, 0))]
        + [pl.BlockSpec((1, 192, 512), lambda k: (k, 0, 0))] * len(packets),
        out_specs=whole((512, 768)),
        scratch_shapes=[pltpu.VMEM((768, 512), F32)],
        compiler_params=params(),
        cost_estimate=LIGHT,
        name="input_grad",
    )(base, weights, *packets)


def body(
    tokens, cotangent, lengths, query_weight, key_weight, value_weight, query_bias, value_bias, output_weight,
    output_bias, first_gain, first_shift, inner_weight, inner_bias, outer_weight, outer_bias, second_gain, second_shift,
):
    n = lax.axis_size("dp")
    me = lax.axis_index("dp")
    rows = query_weight.shape[0]
    heads = query_weight.shape[1] // HD
    few, units = inner_bias.shape
    z = lax.axis_index("tensor")
    slots = jnp.arange(4) ^ z
    counts = jnp.clip(lengths[0] - slots * 512, 0, 512).astype(jnp.int32)
    place = jnp.stack([me & 1, me >> 1, z]).astype(jnp.int32)

    by_head = lambda w: w.reshape(rows, heads, HD)
    wide = jnp.stack(
        [by_head(query_weight), by_head(output_weight), by_head(key_weight), by_head(value_weight)], axis=2
    ).reshape(rows, heads * 256)
    small = jnp.stack([output_bias, first_gain, first_shift, outer_bias, second_gain, second_shift], axis=1)
    biases = jnp.pad(jnp.concatenate([query_bias, value_bias], axis=1), ((0, rows - few), (0, 0)))
    used = 6 + 2 * heads
    near = jnp.concatenate([wide, small, biases, jnp.zeros((rows, 128 - used), BF)], axis=1)

    extra = jnp.pad(inner_bias, ((0, rows - few), (0, 64 - units)))
    front = jnp.concatenate([inner_weight, outer_weight, output_weight, extra], axis=1)
    apart = aligned(rows)
    also = lambda a, m: jnp.concatenate([a, swap(a, "dp", m)], axis=0) if apart else a
    up, down = [tokens], [tokens]

    def hop():
        up.append(shift(up[-1], 1))
        down.append(shift(down[-1], -1))

    hop()
    near = also(near, 2)
    near, up[1], down[1], front = stage(near, up[1], down[1], front)
    front = gather_all(front)
    hop()
    near = also(near, 4)
    later = jnp.concatenate([query_weight, key_weight, value_weight, jnp.zeros((rows, 64), BF)], axis=1)
    near, up[2], down[2], later = stage(near, up[2], down[2], later)
    full = gather_all(later)
    hop()
    if apart:
        at = [me ^ m for m in (0, 2, 4, 6, 1, 3, 5, 7)]
        near, where = [near, swap(near, "dp", 1)], jnp.stack(at).astype(jnp.int32) * rows
    else:
        near, where = [gather_rows(near)], jnp.zeros((1,), jnp.int32)
    tile = assemble(near, where, 128, 6).astype(F32)
    vec = jnp.pad(tile[:, :6].T, ((0, 2), (0, 0)))
    tile = tile.reshape(n, rows, 128)[:, :few, 6:used].reshape(HD, used - 6).T
    blank = jnp.zeros((heads, 2 * HD), F32)
    bias = jnp.concatenate([tile[:heads], blank, tile[heads:]], axis=1)[:, None, :]
    xs = [by_slot(up, down, k) for k in range(3)]
    made = [project(x, (near, where), bias) for x in xs]
    made, up[3], down[3] = stage(made, up[3], down[3])
    xs.append(by_slot(up, down, 3))
    made.append(project(xs[3], (near, where), bias))
    qt, q, kv, kvt = ([m[i] for m in made] for i in range(4))

    mixed, lses = [None] * 4, [None] * 4
    for s in (3, 2, 1, 0):
        mixed[s], lses[s] = attend(counts, qt[s], kv, kvt)
        if s:
            come = mixed[s + 1] if s < 3 else ()
            mixed[s], qt[s - 1], come = stage(mixed[s], qt[s - 1], come)
            if s < 3:
                mixed[s + 1] = come
            mixed[s] = swap(mixed[s], "tensor", s)
    mixed, front = stage(mixed, front)

    sc = jnp.concatenate([counts, place])
    out, g1, d_out, dw = middle(sc, mixed, tokens, cotangent, vec, front, few)

    d = exchange(d_out)
    dq0, dkv, bias0 = back_own(sc, qt[0], q[0], kv, kvt, d_out, lses[0])
    dw, full, bias0 = stage(dw, full, bias0)
    total = lax.psum_scatter(dw, "dp", scatter_dimension=0, tiled=True)
    d, dq0, dkv, bias0 = stage(d, dq0, dkv, bias0)
    head = lambda h, d: back_head(h, sc, qt, q, kv, kvt, d, lses[1:], dq0, dkv, bias0, xs, few)
    packet0, *dw0 = head(0, d)
    packet0, dw0, d = stage(packet0, dw0, d)
    packet0 = exchange(packet0)
    packet1, *dw1 = head(1, d)
    packet0, packet1, dw1, d = stage(packet0, packet1, dw1, d)
    packet1 = exchange(packet1)
    packet2, *dw2 = head(2, d)
    packet1, packet2, dw2 = stage(packet1, packet2, dw2)

    packet2 = exchange(packet2)
    dws = [dw0, dw1, dw2]
    joined = lambda arrays: jnp.concatenate(arrays, axis=-1)
    if apart:
        keep, got = joined([v[0] for v in dws]), swap(joined([v[1] for v in dws]), "dp", 1)
        block = lambda m: keep[m].astype(F32) + got[m].astype(F32)
        passed = swap(jnp.stack([block(1), block(3)]).astype(BF), "dp", 2)
        near_by = (block(2) + passed[1].astype(F32)).astype(BF)
        own = block(0) + passed[0].astype(F32)
    else:
        own, near_by = joined([v[0] for v in dws]), ()
    ahead = input_grad(g1, full, [packet0, packet1], (0, 1))
    ahead, own, near_by, total = stage(ahead, own, near_by, total)
    slots = [total[:, k * 1792 : k * 1792 + 1792] for k in range(4)]
    moved = [swap(v, "tensor", k) for k, v in enumerate(slots) if k]
    own = own + swap(near_by, "dp", 4).astype(F32) if apart else sum_rows(own)
    tokens_grad = input_grad(ahead, full, [packet2], (2,))
    side = lambda i: jnp.concatenate([own[:, h * 256 + i * HD : h * 256 + i * HD + HD] for h in range(heads)], axis=1)
    sides = [side(i) for i in range(3)]
    qb = jnp.stack([own[:few, h * 256 + 192] for h in range(heads)], axis=1)
    vb = jnp.stack([own[:few, h * 256 + 193] for h in range(heads)], axis=1)
    tokens_grad, sides, qb, vb, moved = stage(tokens_grad, sides, qb, vb, moved)

    sums = (slots[0].astype(F32) + moved[0].astype(F32)) + (moved[1].astype(F32) + moved[2].astype(F32))
    ffn, rest = sums[:, :1536], sums[:, 1536:]
    return (
        out,
        tokens_grad,
        *sides,
        qb,
        vb,
        rest[:, :192],
        rest[:, 192],
        rest[:, 193],
        rest[:, 194],
        ffn[:, :768],
        rest[:few, 200 : 200 + units],
        ffn[:, 768:],
        rest[:, 195],
        rest[:, 196],
        rest[:, 197],
    )


def solution(mesh):
    table, vector, token = P("dp", "tensor"), P("dp"), P(("dp", "tensor"), None)
    return jax.shard_map(
        body,
        mesh=mesh,
        in_specs=(
            token, token, vector, table, table, table, table, table, table,
            vector, vector, vector, table, table, table, vector, vector, vector,
        ),
        out_specs=(
            token, token, table, table, table, table, table, table,
            vector, vector, vector, table, table, table, vector, vector, vector,
        ),
        check_vma=False,
    )
```
